128 devices in a mesh: tm: 32 (over y, x, core), blk: 4 (over z).
Axes of the slice: x: 4, y: 4, z: 4, core: 2. Of those that a mesh axis runs over, the one named last changes fastest.
Arguments:
- dynamics: float32 [256, 256], replicated
- dynamics_mask: int32 [8, 8], replicated, may hold values from 0 to 1, as said below
- obs_op: float32 [256, 256], replicated, may hold values from -0.375 to 0.375
- obs_mask: int32 [8, 8], replicated, may hold values from 0 to 1, as said below
- process_noise: float32 [256], replicated, may hold values from 0.0005 to 0.005
- initial_expectation: float32 [256], replicated, may hold values from -6 to 6
- filter_gains: float32 [512, 256, 256], P('tm', 'blk'), may hold values from -0.009765625 to 0.009765625
- observations: float32 [512, 256], P('tm'), may hold values from -6 to 6
- smooth_gains: float32 [512, 256, 256], P('tm', 'blk')
- filt_cov: float32 [512, 256, 256], P('tm', 'blk')
Outputs:
- smoothed_means: float32 [512, 256], P('tm', 'blk')
- smoothed_cov: float32 [512, 256, 256], P('tm', 'blk')
The draws below stay inside these ranges and needn't reach their ends.
Inputs may be any that keep to these rules, and one draw needn't show every extreme that they name: `dynamics_mask`: diagonal blocks are 1. `obs_mask`: blocks with equal row and column index are 1.
All inputs are finite; a program needn't handle non-finite values.
Results may differ from the reference program's by a relative error of at most 0.0003.
Values sent between devices are 32-bit elements; how exact they have to be, the bound alone decides.
A program may use at most 256 MiB of HBM per device.

```python
import math
import jax
import jax.numpy as jnp
from jax import lax

S = 256
OBS = 256
NBLK = 8
OBLK = 8
HORIZON_LENGTH = 512


def draw_dynamics(key, part):
    frequency_seed, displacement_seed = jax.random.split(key)
    rates = jnp.exp(jax.random.uniform(frequency_seed, (S,), jnp.float32, jnp.log(0.5 / HORIZON_LENGTH), jnp.log(0.05)))
    coupling = jax.random.normal(displacement_seed, (S, S), jnp.float32) * (0.25 / (S * HORIZON_LENGTH) ** 0.5)
    return jnp.diag(jnp.exp(-rates)) + coupling - coupling.T


def draw_dynamics_mask(key, part):
    pattern = jax.random.randint(jax.random.fold_in(key, 101), (NBLK, NBLK), 0, 2, jnp.int32)
    return jnp.maximum(pattern, jnp.eye(NBLK, dtype=jnp.int32))


def draw_obs_mask(key, part):
    pattern = jax.random.randint(jax.random.fold_in(key, 202), (OBLK, NBLK), 0, 2, jnp.int32)
    return jnp.maximum(pattern, jnp.eye(OBLK, NBLK, dtype=jnp.int32))


def draw_smooth_gains(key, part):
    frequency_seed, displacement_seed, spike_seed = jax.random.split(key, 3)
    rates = jnp.exp(jax.random.uniform(frequency_seed, (S,), jnp.float32, jnp.log(0.5 / HORIZON_LENGTH), jnp.log(0.05)))
    spike_instant = jax.random.randint(spike_seed, (4,), 0, HORIZON_LENGTH, jnp.int32)
    zeroed_elements = jnp.any(jnp.arange(HORIZON_LENGTH)[:, None] == spike_instant[None, :], axis=1)
    level = jnp.where(zeroed_elements, 0.6, 1.0).astype(jnp.float32)
    coupling = jax.random.normal(displacement_seed, (HORIZON_LENGTH, S, S), jnp.float32) * (0.5 / (S * HORIZON_LENGTH) ** 0.5)
    diagonal_entries = jnp.eye(S, dtype=jnp.float32)[None] * (level[:, None, None] * jnp.exp(-rates)[None, None, :])
    return diagonal_entries + coupling - jnp.swapaxes(coupling, 1, 2)


def draw_filt_cov(key, part):
    key_diag, displacement_seed = jax.random.split(key)
    scales = jnp.exp(jax.random.uniform(key_diag, (HORIZON_LENGTH, S), jnp.float32, jnp.log(0.3), jnp.log(3.0)))
    coupling = jax.random.normal(displacement_seed, (HORIZON_LENGTH, S, S), jnp.float32) * 0.014
    diagonal_entries = jnp.eye(S, dtype=jnp.float32)[None] * scales[:, None, :]
    return diagonal_entries + coupling + jnp.swapaxes(coupling, 1, 2)


def block_scale(own_key, extent, cuts, smallest, top_value):
    def one(position, parts):
        draws = jax.random.uniform(jax.random.fold_in(jax.random.fold_in(own_key, 6), position), (parts,), jnp.float32, smallest / len(cuts), top_value / len(cuts))
        return jnp.repeat(jnp.exp(draws), extent[position] // parts).reshape((-1,) + (1,) * (len(extent) - position - 1))

    gain = one(*cuts[0])
    for cut in cuts[1:]:
        gain = gain * one(*cut)
    return gain


def scatter_about(stream_key, shape, spread, limit, cuts=(), kind=jnp.bfloat16):
    result = jax.random.normal(stream_key, shape, jnp.float32) * spread
    if len(cuts) > 0:
        result = block_scale(stream_key, shape, cuts, -0.22, 0.18) * result
    return jnp.clip(result, min=-limit, max=limit).astype(kind)


def setup_inputs(seed: int = 0) -> dict:
    streams_of = jax.random.split(jax.random.key(seed), 11)
    dynamics = draw_dynamics(jax.random.fold_in(streams_of[10], 71), 0)
    dynamics_mask = draw_dynamics_mask(jax.random.fold_in(streams_of[10], 71), 0)
    obs_op = scatter_about(streams_of[2], (OBS, S), S ** -0.5, 0.375, (), jnp.float32)
    obs_mask = draw_obs_mask(jax.random.fold_in(streams_of[10], 71), 0)
    process_noise = jnp.clip(jnp.exp(jax.random.uniform(streams_of[4], (S,), jnp.float32, math.log(0.0005), math.log(0.005))), 0.0005, 0.005)
    initial_expectation = scatter_about(streams_of[5], (S,), 1.0, 6.0, (), jnp.float32)
    filter_gains = scatter_about(streams_of[6], (HORIZON_LENGTH, S, OBS), (HORIZON_LENGTH * 625) ** -0.5, 0.009765625, ((0, 32), (1, 4)), jnp.float32)
    observations = scatter_about(streams_of[7], (HORIZON_LENGTH, OBS), 1.0, 6.0, ((0, 32),), jnp.float32)
    smooth_gains = draw_smooth_gains(jax.random.fold_in(streams_of[10], 71), 0)
    filt_cov = draw_filt_cov(jax.random.fold_in(streams_of[10], 71), 0)
    return {"dynamics": dynamics, "dynamics_mask": dynamics_mask, "obs_op": obs_op, "obs_mask": obs_mask, "process_noise": process_noise, "initial_expectation": initial_expectation, "filter_gains": filter_gains, "observations": observations, "smooth_gains": smooth_gains, "filt_cov": filt_cov}


highest = lax.Precision.HIGHEST


def expand_mask(mask, row_total, col_total):
    row_block = row_total // mask.shape[0]
    col_block = col_total // mask.shape[1]
    return jnp.repeat(jnp.repeat(mask.astype(jnp.float32), row_block, axis=0), col_block, axis=1)


def reference(dynamics, dynamics_mask, obs_op, obs_mask, process_noise, initial_expectation, filter_gains, observations, smooth_gains, filt_cov):
    trans_map = dynamics * expand_mask(dynamics_mask, S, S)
    obs_map = obs_op * expand_mask(obs_mask, OBS, S)
    obs_dyn = jnp.dot(obs_map, trans_map, precision=highest)

    def filter_step(current, inputs):
        gain_now, seen_now = inputs
        step_map = trans_map - jnp.dot(gain_now, obs_dyn, precision=highest)
        step_shift = jnp.dot(gain_now, seen_now, precision=highest)
        current = jnp.dot(step_map, current, precision=highest) + step_shift
        return current, current

    filt_means = lax.scan(filter_step, initial_expectation, (filter_gains, observations))[1]
    final_step = jnp.arange(HORIZON_LENGTH) == HORIZON_LENGTH - 1
    gain_all = jnp.where(final_step[:, None, None], jnp.float32(0.0), smooth_gains)

    def smooth_step(current, inputs):
        cov_next, mean_next = current
        gain_now, cov_filt, mean_filt = inputs
        predicted = jnp.dot(jnp.dot(trans_map, cov_filt, precision=highest), trans_map.T, precision=highest) + jnp.diag(process_noise)
        residual = cov_filt - jnp.dot(jnp.dot(gain_now, predicted, precision=highest), gain_now.T, precision=highest)
        offset = mean_filt - jnp.dot(gain_now, jnp.dot(trans_map, mean_filt, precision=highest), precision=highest)
        cov_now = jnp.dot(jnp.dot(gain_now, cov_next, precision=highest), gain_now.T, precision=highest) + residual
        current_mean = jnp.dot(gain_now, mean_next, precision=highest) + offset
        return (cov_now, current_mean), (current_mean, cov_now)

    start_state = (jnp.zeros((S, S), jnp.float32), jnp.zeros((S,), jnp.float32))
    results = lax.scan(smooth_step, start_state, (gain_all, filt_cov, filt_means), reverse=True)[1]
    return results[0], results[1]
```

```python
import jax
import jax.numpy as jnp
from jax import lax
from jax.sharding import PartitionSpec as P

highest = lax.Precision.HIGHEST


def from_behind(block, axis, distance):
    devices = range(lax.axis_size(axis))
    route = [(i - distance, i) for i in devices if i - distance in devices]
    return lax.ppermute(block, axis, route)


def expand_mask(mask, row_total, col_total):
    row_block = row_total // mask.shape[0]
    col_block = col_total // mask.shape[1]
    return jnp.repeat(jnp.repeat(mask.astype(jnp.float32), row_block, axis=0), col_block, axis=1)


def matmul(left, right):
    return jnp.matmul(left, right, precision=highest)


def matvec(left, right):
    return jnp.einsum("...ij,...j->...i", left, right, precision=highest)


def transpose(mats):
    return jnp.swapaxes(mats, -1, -2)


def filter_tree(maps, shifts):
    while maps.shape[0] > 1:
        early_map, late_map = maps[0::2], maps[1::2]
        shifts = matvec(late_map, shifts[0::2]) + shifts[1::2]
        maps = matmul(late_map, early_map)
    return maps[0], shifts[0]


def smooth_tree(gains, resids, offsets):
    while gains.shape[0] > 1:
        outer, inner = gains[0::2], gains[1::2]
        resids = matmul(matmul(outer, resids[1::2]), transpose(outer)) + resids[0::2]
        offsets = matvec(outer, offsets[1::2]) + offsets[0::2]
        gains = matmul(outer, inner)
    return gains[0], resids[0], offsets[0]


def filter_scan(window_map, window_shift, initial_expectation, tm_index, tm_count):
    width = window_map.shape[0]
    first_window = tm_index == 0
    shift = jnp.where(first_window, matvec(window_map, initial_expectation) + window_shift, window_shift)
    cmap = jnp.where(first_window, jnp.float32(0.0), window_map)
    distance = 1
    while distance < tm_count:
        has_left = tm_index >= distance
        if 2 * distance >= tm_count:
            shift_left = from_behind(shift, "tm", distance)
            shift = jnp.where(has_left, matvec(cmap, shift_left) + shift, shift)
        else:
            arrived = from_behind(jnp.concatenate([cmap, shift[None]], axis=0), "tm", distance)
            map_left, shift_left = arrived[:width], arrived[width]
            shift = jnp.where(has_left, matvec(cmap, shift_left) + shift, shift)
            cmap = jnp.where(has_left, matmul(cmap, map_left), cmap)
        distance *= 2
    mean_in = from_behind(shift, "tm", 1)
    return jnp.where(first_window, initial_expectation, mean_in)


def smooth_scan(window_gain, window_resid, window_offset, tm_index, tm_count):
    width = window_gain.shape[0]
    gain, resid, offset = window_gain, window_resid, window_offset
    distance = 1
    while distance < tm_count:
        has_right = tm_index + distance < tm_count
        if 2 * distance >= tm_count:
            arrived = from_behind(jnp.concatenate([resid, offset[None]], axis=0), "tm", -distance)
            resid_right, offset_right = arrived[:width], arrived[width]
        else:
            arrived = from_behind(
                jnp.concatenate([gain, resid, offset[None]], axis=0), "tm", -distance
            )
            gain_right = arrived[:width]
            resid_right = arrived[width : 2 * width]
            offset_right = arrived[2 * width]
        new_resid = matmul(matmul(gain, resid_right), gain.T) + resid
        offset = jnp.where(has_right, matvec(gain, offset_right) + offset, offset)
        resid = jnp.where(has_right, new_resid, resid)
        if 2 * distance < tm_count:
            gain = jnp.where(has_right, matmul(gain, gain_right), gain)
        distance *= 2
    arrived = from_behind(jnp.concatenate([resid, offset[None]], axis=0), "tm", -1)
    last_window = tm_index == tm_count - 1
    arrived = jnp.where(last_window, jnp.float32(0.0), arrived)
    return arrived[:width], arrived[width]


def window_work(
    trans_map,
    process_noise,
    initial_expectation,
    transition_operators,
    step_shifts,
    gain_full,
    cov_full,
    tm_index,
    tm_count,
):
    step_count = transition_operators.shape[0]
    final_step = jnp.logical_and(tm_index == tm_count - 1, jnp.arange(step_count) == step_count - 1)
    gain_full = jnp.where(final_step[:, None, None], jnp.float32(0.0), gain_full)

    window_map, window_shift = filter_tree(transition_operators, step_shifts)
    mean_in = filter_scan(window_map, window_shift, initial_expectation, tm_index, tm_count)

    def filter_walk(current, step_parts):
        current = matmul(step_parts[0], current) + step_parts[1]
        return (current, current)

    filt_means = lax.scan(filter_walk, mean_in, (transition_operators, step_shifts))[1]
    predicted = matmul(matmul(trans_map, cov_full), trans_map.T) + jnp.diag(process_noise)
    gain_trans = jnp.swapaxes(gain_full, 1, 2)
    residual_cov = cov_full - matmul(matmul(gain_full, predicted), gain_trans)
    moved_means = jnp.einsum("ij,tj->ti", trans_map, filt_means, precision=highest)
    offsets = filt_means - jnp.einsum("tij,tj->ti", gain_full, moved_means, precision=highest)

    window_gain, window_resid, window_offset = smooth_tree(gain_full, residual_cov, offsets)
    cov_after, mean_after = smooth_scan(window_gain, window_resid, window_offset, tm_index, tm_count)

    def smooth_walk(current, step_parts):
        cov_next, mean_next = current
        gain_now, resid_now, offset_now = step_parts
        cov_now = matmul(matmul(gain_now, cov_next), gain_now.T) + resid_now
        current_mean = matmul(gain_now, mean_next) + offset_now
        return ((cov_now, current_mean), (current_mean, cov_now))

    return lax.scan(
        smooth_walk,
        (cov_after, mean_after),
        (gain_full, residual_cov, offsets),
        reverse=True,
    )[1]


def per_device(
    dynamics,
    dynamics_mask,
    obs_op,
    obs_mask,
    process_noise,
    initial_expectation,
    filter_gains,
    observations,
    smooth_gains,
    filt_cov,
):
    width = dynamics.shape[0]
    obs_width = obs_op.shape[0]
    row_count = filter_gains.shape[1]
    row_start = lax.axis_index("blk") * row_count
    trans_map = dynamics * expand_mask(dynamics_mask, width, width)
    obs_map = obs_op * expand_mask(obs_mask, obs_width, width)
    obs_dyn = matmul(obs_map, trans_map)
    own_rows = lax.dynamic_slice_in_dim(trans_map, row_start, row_count, 0)
    map_rows = own_rows[None] - matmul(filter_gains, obs_dyn)
    shift_rows = jnp.einsum("tro,to->tr", filter_gains, observations, precision=highest)
    transition_operators, step_shifts, gain_full, cov_full = (
        lax.all_gather(map_rows, "blk", axis=1, tiled=True),
        lax.all_gather(shift_rows, "blk", axis=1, tiled=True),
        lax.all_gather(smooth_gains, "blk", axis=1, tiled=True),
        lax.all_gather(filt_cov, "blk", axis=1, tiled=True),
    )
    means_out, cov_out = window_work(
        trans_map,
        process_noise,
        initial_expectation,
        transition_operators,
        step_shifts,
        gain_full,
        cov_full,
        lax.axis_index("tm"),
        lax.axis_size("tm"),
    )
    means_rows = lax.dynamic_slice_in_dim(means_out, row_start, row_count, 1)
    cov_rows = lax.dynamic_slice_in_dim(cov_out, row_start, row_count, 1)
    return (means_rows, cov_rows)


def solution(mesh):
    return jax.shard_map(
        per_device,
        mesh=mesh,
        in_specs=(
            P(),
            P(),
            P(),
            P(),
            P(),
            P(),
            P("tm", "blk", None),
            P("tm", None),
            P("tm", "blk", None),
            P("tm", "blk", None),
        ),
        out_specs=(P("tm", "blk"), P("tm", "blk", None)),
        check_vma=False,
    )
```

```python
import jax
import jax.numpy as jnp
from jax import lax
from jax.sharding import PartitionSpec as P

highest = lax.Precision.HIGHEST
CHUNKS = ("tm", "blk")


def from_behind(block, axis, distance):
    devices = range(lax.axis_size(axis))
    route = [(i - distance, i) for i in devices if i - distance in devices]
    return lax.ppermute(block, axis, route)


def expand_mask(mask, row_total, col_total):
    row_block = row_total // mask.shape[0]
    col_block = col_total // mask.shape[1]
    return jnp.repeat(jnp.repeat(mask.astype(jnp.float32), row_block, axis=0), col_block, axis=1)


def matmul(left, right):
    return jnp.matmul(left, right, precision=highest)


def matvec(left, right):
    return jnp.einsum("...ij,...j->...i", left, right, precision=highest)


def transpose(mats):
    return jnp.swapaxes(mats, -1, -2)


def filter_tree(maps, shifts):
    while maps.shape[0] > 1:
        early_map, late_map = maps[0::2], maps[1::2]
        shifts = matvec(late_map, shifts[0::2]) + shifts[1::2]
        maps = matmul(late_map, early_map)
    return maps[0], shifts[0]


def smooth_tree(gains, resids, offsets):
    while gains.shape[0] > 1:
        outer, inner = gains[0::2], gains[1::2]
        resids = matmul(matmul(outer, resids[1::2]), transpose(outer)) + resids[0::2]
        offsets = matvec(outer, offsets[1::2]) + offsets[0::2]
        gains = matmul(outer, inner)
    return gains[0], resids[0], offsets[0]


def filter_scan(window_map, window_shift, initial_expectation, tm_index, tm_count):
    width = window_map.shape[0]
    first_window = tm_index == 0
    shift = jnp.where(first_window, matvec(window_map, initial_expectation) + window_shift, window_shift)
    cmap = jnp.where(first_window, jnp.float32(0.0), window_map)
    distance = 1
    while distance < tm_count:
        has_left = tm_index >= distance
        if 2 * distance >= tm_count:
            shift_left = from_behind(shift, CHUNKS, distance)
            shift = jnp.where(has_left, matvec(cmap, shift_left) + shift, shift)
        else:
            arrived = from_behind(jnp.concatenate([cmap, shift[None]], axis=0), CHUNKS, distance)
            map_left, shift_left = arrived[:width], arrived[width]
            shift = jnp.where(has_left, matvec(cmap, shift_left) + shift, shift)
            cmap = jnp.where(has_left, matmul(cmap, map_left), cmap)
        distance *= 2
    mean_in = from_behind(shift, CHUNKS, 1)
    return jnp.where(first_window, initial_expectation, mean_in)


def smooth_scan(window_gain, window_resid, window_offset, tm_index, tm_count):
    width = window_gain.shape[0]
    gain, resid, offset = window_gain, window_resid, window_offset
    distance = 1
    while distance < tm_count:
        has_right = tm_index + distance < tm_count
        if 2 * distance >= tm_count:
            arrived = from_behind(jnp.concatenate([resid, offset[None]], axis=0), CHUNKS, -distance)
            resid_right, offset_right = arrived[:width], arrived[width]
        else:
            arrived = from_behind(
                jnp.concatenate([gain, resid, offset[None]], axis=0), CHUNKS, -distance
            )
            gain_right = arrived[:width]
            resid_right = arrived[width : 2 * width]
            offset_right = arrived[2 * width]
        new_resid = matmul(matmul(gain, resid_right), gain.T) + resid
        offset = jnp.where(has_right, matvec(gain, offset_right) + offset, offset)
        resid = jnp.where(has_right, new_resid, resid)
        if 2 * distance < tm_count:
            gain = jnp.where(has_right, matmul(gain, gain_right), gain)
        distance *= 2
    arrived = from_behind(jnp.concatenate([resid, offset[None]], axis=0), CHUNKS, -1)
    last_window = tm_index == tm_count - 1
    arrived = jnp.where(last_window, jnp.float32(0.0), arrived)
    return arrived[:width], arrived[width]


def window_work(
    trans_map,
    process_noise,
    initial_expectation,
    transition_operators,
    step_shifts,
    gain_full,
    cov_full,
    tm_index,
    tm_count,
):
    step_count = transition_operators.shape[0]
    final_step = jnp.logical_and(tm_index == tm_count - 1, jnp.arange(step_count) == step_count - 1)
    gain_full = jnp.where(final_step[:, None, None], jnp.float32(0.0), gain_full)

    window_map, window_shift = filter_tree(transition_operators, step_shifts)
    mean_in = filter_scan(window_map, window_shift, initial_expectation, tm_index, tm_count)

    def filter_walk(current, step_parts):
        current = matmul(step_parts[0], current) + step_parts[1]
        return (current, current)

    filt_means = lax.scan(filter_walk, mean_in, (transition_operators, step_shifts))[1]
    predicted = matmul(matmul(trans_map, cov_full), trans_map.T) + jnp.diag(process_noise)
    gain_trans = jnp.swapaxes(gain_full, 1, 2)
    residual_cov = cov_full - matmul(matmul(gain_full, predicted), gain_trans)
    moved_means = jnp.einsum("ij,tj->ti", trans_map, filt_means, precision=highest)
    offsets = filt_means - jnp.einsum("tij,tj->ti", gain_full, moved_means, precision=highest)

    window_gain, window_resid, window_offset = smooth_tree(gain_full, residual_cov, offsets)
    cov_after, mean_after = smooth_scan(window_gain, window_resid, window_offset, tm_index, tm_count)

    def smooth_walk(current, step_parts):
        cov_next, mean_next = current
        gain_now, resid_now, offset_now = step_parts
        cov_now = matmul(matmul(gain_now, cov_next), gain_now.T) + resid_now
        current_mean = matmul(gain_now, mean_next) + offset_now
        return ((cov_now, current_mean), (current_mean, cov_now))

    return lax.scan(
        smooth_walk,
        (cov_after, mean_after),
        (gain_full, residual_cov, offsets),
        reverse=True,
    )[1]


def per_device(
    dynamics,
    dynamics_mask,
    obs_op,
    obs_mask,
    process_noise,
    initial_expectation,
    filter_gains,
    observations,
    smooth_gains,
    filt_cov,
):
    width = dynamics.shape[0]
    obs_width = obs_op.shape[0]
    row_count = filter_gains.shape[1]
    row_start = lax.axis_index("blk") * row_count
    trans_map = dynamics * expand_mask(dynamics_mask, width, width)
    obs_map = obs_op * expand_mask(obs_mask, obs_width, width)
    obs_dyn = matmul(obs_map, trans_map)
    own_rows = lax.dynamic_slice_in_dim(trans_map, row_start, row_count, 0)
    map_rows = own_rows[None] - matmul(filter_gains, obs_dyn)
    shift_rows = jnp.einsum("tro,to->tr", filter_gains, observations, precision=highest)
    def steps_whole(rows):
        return lax.all_to_all(rows, "blk", 0, 1, tiled=True)

    def rows_of_steps(whole):
        return lax.all_to_all(whole, "blk", 1, 0, tiled=True)

    means_out, cov_out = window_work(
        trans_map,
        process_noise,
        initial_expectation,
        steps_whole(map_rows),
        steps_whole(shift_rows),
        steps_whole(smooth_gains),
        steps_whole(filt_cov),
        lax.axis_index(CHUNKS),
        lax.axis_size(CHUNKS),
    )
    return (rows_of_steps(means_out), rows_of_steps(cov_out))


def solution(mesh):
    return jax.shard_map(
        per_device,
        mesh=mesh,
        in_specs=(
            P(),
            P(),
            P(),
            P(),
            P(),
            P(),
            P("tm", "blk", None),
            P("tm", None),
            P("tm", "blk", None),
            P("tm", "blk", None),
        ),
        out_specs=(P("tm", "blk"), P("tm", "blk", None)),
        check_vma=False,
    )
```

```python
import jax
import jax.numpy as jnp
from jax import lax
from jax.sharding import PartitionSpec as P

highest = lax.Precision.HIGHEST
CHUNKS = ("tm", "blk")


def from_behind(block, axis, distance):
    devices = range(lax.axis_size(axis))
    route = [(i - distance, i) for i in devices if i - distance in devices]
    return lax.ppermute(block, axis, route)


def expand_mask(mask, row_total, col_total):
    row_block = row_total // mask.shape[0]
    col_block = col_total // mask.shape[1]
    return jnp.repeat(jnp.repeat(mask.astype(jnp.float32), row_block, axis=0), col_block, axis=1)


def matmul(left, right):
    return jnp.matmul(left, right, precision=highest)


def matvec(left, right):
    return jnp.einsum("...ij,...j->...i", left, right, precision=highest)


def transpose(mats):
    return jnp.swapaxes(mats, -1, -2)


def filter_tree(maps, shifts):
    while maps.shape[0] > 1:
        early_map, late_map = maps[0::2], maps[1::2]
        shifts = matvec(late_map, shifts[0::2]) + shifts[1::2]
        maps = matmul(late_map, early_map)
    return maps[0], shifts[0]


def smooth_tree(gains, resids, offsets):
    while gains.shape[0] > 1:
        outer, inner = gains[0::2], gains[1::2]
        resids = matmul(matmul(outer, resids[1::2]), transpose(outer)) + resids[0::2]
        offsets = matvec(outer, offsets[1::2]) + offsets[0::2]
        gains = matmul(outer, inner)
    return gains[0], resids[0], offsets[0]


def filter_scan(window_map, window_shift, initial_expectation, tm_index, tm_count):
    width = window_map.shape[0]
    first_window = tm_index == 0
    shift = jnp.where(first_window, matvec(window_map, initial_expectation) + window_shift, window_shift)
    cmap = jnp.where(first_window, jnp.float32(0.0), window_map)
    distance = 1
    while distance < tm_count:
        has_left = tm_index >= distance
        if 2 * distance >= tm_count:
            shift_left = from_behind(shift, CHUNKS, distance)
            shift = jnp.where(has_left, matvec(cmap, shift_left) + shift, shift)
        else:
            arrived = from_behind(jnp.concatenate([cmap, shift[None]], axis=0), CHUNKS, distance)
            map_left, shift_left = arrived[:width], arrived[width]
            shift = jnp.where(has_left, matvec(cmap, shift_left) + shift, shift)
            cmap = jnp.where(has_left, matmul(cmap, map_left), cmap)
        distance *= 2
    mean_in = from_behind(shift, CHUNKS, 1)
    return jnp.where(first_window, initial_expectation, mean_in)


def smooth_scan(window_gain, window_resid, window_offset, tm_index, tm_count):
    width = window_gain.shape[0]
    gain, resid, offset = window_gain, window_resid, window_offset
    distance = 1
    while distance < tm_count:
        has_right = tm_index + distance < tm_count
        if 2 * distance >= tm_count:
            arrived = from_behind(jnp.concatenate([resid, offset[None]], axis=0), CHUNKS, -distance)
            resid_right, offset_right = arrived[:width], arrived[width]
        else:
            arrived = from_behind(
                jnp.concatenate([gain, resid, offset[None]], axis=0), CHUNKS, -distance
            )
            gain_right = arrived[:width]
            resid_right = arrived[width : 2 * width]
            offset_right = arrived[2 * width]
        new_resid = matmul(matmul(gain, resid_right), gain.T) + resid
        offset = jnp.where(has_right, matvec(gain, offset_right) + offset, offset)
        resid = jnp.where(has_right, new_resid, resid)
        if 2 * distance < tm_count:
            gain = jnp.where(has_right, matmul(gain, gain_right), gain)
        distance *= 2
    arrived = from_behind(jnp.concatenate([resid, offset[None]], axis=0), CHUNKS, -1)
    last_window = tm_index == tm_count - 1
    arrived = jnp.where(last_window, jnp.float32(0.0), arrived)
    return arrived[:width], arrived[width]


def window_work(
    trans_map,
    process_noise,
    initial_expectation,
    transition_operators,
    step_shifts,
    gain_full,
    cov_full,
    tm_index,
    tm_count,
):
    step_count = transition_operators.shape[0]
    final_step = jnp.logical_and(tm_index == tm_count - 1, jnp.arange(step_count) == step_count - 1)
    gain_full = jnp.where(final_step[:, None, None], jnp.float32(0.0), gain_full)

    window_map, window_shift = filter_tree(transition_operators, step_shifts)
    mean_in = filter_scan(window_map, window_shift, initial_expectation, tm_index, tm_count)

    filt_steps = []
    current = mean_in
    for step in range(step_count):
        current = matvec(transition_operators[step], current) + step_shifts[step]
        filt_steps.append(current)
    filt_means = jnp.stack(filt_steps)
    predicted = matmul(matmul(trans_map, cov_full), trans_map.T) + jnp.diag(process_noise)
    gain_trans = jnp.swapaxes(gain_full, 1, 2)
    residual_cov = cov_full - matmul(matmul(gain_full, predicted), gain_trans)
    moved_means = jnp.einsum("ij,tj->ti", trans_map, filt_means, precision=highest)
    offsets = filt_means - jnp.einsum("tij,tj->ti", gain_full, moved_means, precision=highest)

    window_gain, window_resid, window_offset = smooth_tree(gain_full, residual_cov, offsets)
    cov_after, mean_after = smooth_scan(window_gain, window_resid, window_offset, tm_index, tm_count)

    cov_steps = [None] * step_count
    mean_steps = [None] * step_count
    cov_next, mean_next = cov_after, mean_after
    for step in reversed(range(step_count)):
        gain_now = gain_full[step]
        cov_next = matmul(matmul(gain_now, cov_next), gain_now.T) + residual_cov[step]
        mean_next = matvec(gain_now, mean_next) + offsets[step]
        cov_steps[step] = cov_next
        mean_steps[step] = mean_next
    return jnp.stack(mean_steps), jnp.stack(cov_steps)


def per_device(
    dynamics,
    dynamics_mask,
    obs_op,
    obs_mask,
    process_noise,
    initial_expectation,
    filter_gains,
    observations,
    smooth_gains,
    filt_cov,
):
    width = dynamics.shape[0]
    obs_width = obs_op.shape[0]
    row_count = filter_gains.shape[1]
    row_start = lax.axis_index("blk") * row_count
    trans_map = dynamics * expand_mask(dynamics_mask, width, width)
    obs_map = obs_op * expand_mask(obs_mask, obs_width, width)
    obs_dyn = matmul(obs_map, trans_map)
    own_rows = lax.dynamic_slice_in_dim(trans_map, row_start, row_count, 0)
    map_rows = own_rows[None] - matmul(filter_gains, obs_dyn)
    shift_rows = jnp.einsum("tro,to->tr", filter_gains, observations, precision=highest)
    def steps_whole(rows):
        return lax.all_to_all(rows, "blk", 0, 1, tiled=True)

    def rows_of_steps(whole):
        return lax.all_to_all(whole, "blk", 1, 0, tiled=True)

    means_out, cov_out = window_work(
        trans_map,
        process_noise,
        initial_expectation,
        steps_whole(map_rows),
        steps_whole(shift_rows),
        steps_whole(smooth_gains),
        steps_whole(filt_cov),
        lax.axis_index(CHUNKS),
        lax.axis_size(CHUNKS),
    )
    return (rows_of_steps(means_out), rows_of_steps(cov_out))


def solution(mesh):
    return jax.shard_map(
        per_device,
        mesh=mesh,
        in_specs=(
            P(),
            P(),
            P(),
            P(),
            P(),
            P(),
            P("tm", "blk", None),
            P("tm", None),
            P("tm", "blk", None),
            P("tm", "blk", None),
        ),
        out_specs=(P("tm", "blk"), P("tm", "blk", None)),
        check_vma=False,
    )
```

```python
import jax
import jax.numpy as jnp
from jax import lax
from jax.experimental import pallas as pl
from jax.experimental.pallas import tpu as pltpu
from jax.sharding import PartitionSpec as P

highest = lax.Precision.HIGHEST
CHUNKS = ("tm", "blk")


MESH = pl.DeviceIdType.MESH
kernel_ids = [0]


def piece_bounds(rows, pieces):
    step = -(-rows // pieces)
    step = -(-step // 8) * 8
    return [(lo, min(lo + step, rows)) for lo in range(0, rows, step)]


def from_behind(block, axis, distance, pieces=4):
    assert axis == CHUNKS
    chunk_count = lax.axis_size(CHUNKS)
    blk_count = lax.axis_size("blk")
    if block.ndim == 1:
        bounds = [(0, block.shape[0])]
    else:
        bounds = piece_bounds(block.shape[0], pieces)
    kernel_ids[0] += 1

    def kernel(x_ref, o_ref, send_sems, recv_sems):
        me = lax.axis_index("tm") * blk_count + lax.axis_index("blk")
        source = me - distance
        target = me + distance
        if distance > 0:
            source_count = (source + chunk_count) // chunk_count
            target_count = 1 - target // chunk_count
        else:
            source_count = 1 - source // chunk_count
            target_count = (target + chunk_count) // chunk_count
        has_source = source_count > 0
        has_target = target_count > 0
        source_id = (source // blk_count, source % blk_count)
        target_id = (target // blk_count, target % blk_count)
        barrier = pltpu.get_barrier_semaphore()

        @pl.when(has_source)
        def _():
            pl.semaphore_signal(barrier, 1, device_id=source_id, device_id_type=MESH)

        @pl.when(has_target)
        def _():
            pl.semaphore_signal(barrier, 1, device_id=target_id, device_id_type=MESH)

        pl.semaphore_wait(barrier, source_count + target_count)

        copies = [
            pltpu.make_async_remote_copy(
                src_ref=x_ref.at[lo:hi],
                dst_ref=o_ref.at[lo:hi],
                send_sem=send_sems.at[k],
                recv_sem=recv_sems.at[k],
                device_id=target_id,
                device_id_type=MESH,
            )
            for k, (lo, hi) in enumerate(bounds)
        ]

        @pl.when(has_target)
        def _():
            for copy in copies:
                copy.start()

        @pl.when(has_source)
        def _():
            for copy in copies:
                copy.wait_recv()

        @pl.when(has_target)
        def _():
            for copy in copies:
                copy.wait_send()

    return pl.pallas_call(
        kernel,
        out_shape=jax.ShapeDtypeStruct(block.shape, block.dtype),
        in_specs=[pl.BlockSpec(memory_space=pl.ANY)],
        out_specs=pl.BlockSpec(memory_space=pl.ANY),
        scratch_shapes=[
            pltpu.SemaphoreType.DMA((len(bounds),)),
            pltpu.SemaphoreType.DMA((len(bounds),)),
        ],
        compiler_params=pltpu.CompilerParams(collective_id=kernel_ids[0], has_side_effects=True),
    )(block)


def expand_mask(mask, row_total, col_total):
    row_block = row_total // mask.shape[0]
    col_block = col_total // mask.shape[1]
    return jnp.repeat(jnp.repeat(mask.astype(jnp.float32), row_block, axis=0), col_block, axis=1)


def matmul(left, right):
    return jnp.matmul(left, right, precision=highest)


def matvec(left, right):
    return jnp.einsum("...ij,...j->...i", left, right, precision=highest)


def transpose(mats):
    return jnp.swapaxes(mats, -1, -2)


def filter_tree(maps, shifts):
    while maps.shape[0] > 1:
        early_map, late_map = maps[0::2], maps[1::2]
        shifts = matvec(late_map, shifts[0::2]) + shifts[1::2]
        maps = matmul(late_map, early_map)
    return maps[0], shifts[0]


def smooth_tree(gains, resids, offsets):
    while gains.shape[0] > 1:
        outer, inner = gains[0::2], gains[1::2]
        resids = matmul(matmul(outer, resids[1::2]), transpose(outer)) + resids[0::2]
        offsets = matvec(outer, offsets[1::2]) + offsets[0::2]
        gains = matmul(outer, inner)
    return gains[0], resids[0], offsets[0]


def filter_scan(window_map, window_shift, initial_expectation, tm_index, tm_count):
    width = window_map.shape[0]
    first_window = tm_index == 0
    shift = jnp.where(first_window, matvec(window_map, initial_expectation) + window_shift, window_shift)
    cmap = jnp.where(first_window, jnp.float32(0.0), window_map)
    distance = 1
    while distance < tm_count:
        has_left = tm_index >= distance
        if 2 * distance >= tm_count:
            shift_left = from_behind(shift, CHUNKS, distance)
            shift = jnp.where(has_left, matvec(cmap, shift_left) + shift, shift)
        else:
            arrived = from_behind(jnp.concatenate([cmap, shift[None]], axis=0), CHUNKS, distance)
            map_left, shift_left = arrived[:width], arrived[width]
            shift = jnp.where(has_left, matvec(cmap, shift_left) + shift, shift)
            cmap = jnp.where(has_left, matmul(cmap, map_left), cmap)
        distance *= 2
    mean_in = from_behind(shift, CHUNKS, 1)
    return jnp.where(first_window, initial_expectation, mean_in)


def smooth_scan(window_gain, window_resid, window_offset, tm_index, tm_count):
    width = window_gain.shape[0]
    gain, resid, offset = window_gain, window_resid, window_offset
    distance = 1
    while distance < tm_count:
        has_right = tm_index + distance < tm_count
        if 2 * distance >= tm_count:
            arrived = from_behind(jnp.concatenate([resid, offset[None]], axis=0), CHUNKS, -distance)
            resid_right, offset_right = arrived[:width], arrived[width]
        else:
            arrived = from_behind(
                jnp.concatenate([gain, resid, offset[None]], axis=0), CHUNKS, -distance
            )
            gain_right = arrived[:width]
            resid_right = arrived[width : 2 * width]
            offset_right = arrived[2 * width]
        new_resid = matmul(matmul(gain, resid_right), gain.T) + resid
        offset = jnp.where(has_right, matvec(gain, offset_right) + offset, offset)
        resid = jnp.where(has_right, new_resid, resid)
        if 2 * distance < tm_count:
            gain = jnp.where(has_right, matmul(gain, gain_right), gain)
        distance *= 2
    arrived = from_behind(jnp.concatenate([resid, offset[None]], axis=0), CHUNKS, -1)
    last_window = tm_index == tm_count - 1
    arrived = jnp.where(last_window, jnp.float32(0.0), arrived)
    return arrived[:width], arrived[width]


def window_work(
    trans_map,
    process_noise,
    initial_expectation,
    transition_operators,
    step_shifts,
    gain_full,
    cov_full,
    tm_index,
    tm_count,
):
    step_count = transition_operators.shape[0]
    final_step = jnp.logical_and(tm_index == tm_count - 1, jnp.arange(step_count) == step_count - 1)
    gain_full = jnp.where(final_step[:, None, None], jnp.float32(0.0), gain_full)

    window_map, window_shift = filter_tree(transition_operators, step_shifts)
    mean_in = filter_scan(window_map, window_shift, initial_expectation, tm_index, tm_count)

    filt_steps = []
    current = mean_in
    for step in range(step_count):
        current = matvec(transition_operators[step], current) + step_shifts[step]
        filt_steps.append(current)
    filt_means = jnp.stack(filt_steps)
    predicted = matmul(matmul(trans_map, cov_full), trans_map.T) + jnp.diag(process_noise)
    gain_trans = jnp.swapaxes(gain_full, 1, 2)
    residual_cov = cov_full - matmul(matmul(gain_full, predicted), gain_trans)
    moved_means = jnp.einsum("ij,tj->ti", trans_map, filt_means, precision=highest)
    offsets = filt_means - jnp.einsum("tij,tj->ti", gain_full, moved_means, precision=highest)

    window_gain, window_resid, window_offset = smooth_tree(gain_full, residual_cov, offsets)
    cov_after, mean_after = smooth_scan(window_gain, window_resid, window_offset, tm_index, tm_count)

    cov_steps = [None] * step_count
    mean_steps = [None] * step_count
    cov_next, mean_next = cov_after, mean_after
    for step in reversed(range(step_count)):
        gain_now = gain_full[step]
        cov_next = matmul(matmul(gain_now, cov_next), gain_now.T) + residual_cov[step]
        mean_next = matvec(gain_now, mean_next) + offsets[step]
        cov_steps[step] = cov_next
        mean_steps[step] = mean_next
    return jnp.stack(mean_steps), jnp.stack(cov_steps)


def per_device(
    dynamics,
    dynamics_mask,
    obs_op,
    obs_mask,
    process_noise,
    initial_expectation,
    filter_gains,
    observations,
    smooth_gains,
    filt_cov,
):
    kernel_ids[0] = 0
    width = dynamics.shape[0]
    obs_width = obs_op.shape[0]
    row_count = filter_gains.shape[1]
    row_start = lax.axis_index("blk") * row_count
    trans_map = dynamics * expand_mask(dynamics_mask, width, width)
    obs_map = obs_op * expand_mask(obs_mask, obs_width, width)
    obs_dyn = matmul(obs_map, trans_map)
    own_rows = lax.dynamic_slice_in_dim(trans_map, row_start, row_count, 0)
    map_rows = own_rows[None] - matmul(filter_gains, obs_dyn)
    shift_rows = jnp.einsum("tro,to->tr", filter_gains, observations, precision=highest)
    def steps_whole(rows):
        return lax.all_to_all(rows, "blk", 0, 1, tiled=True)

    def rows_of_steps(whole):
        return lax.all_to_all(whole, "blk", 1, 0, tiled=True)

    means_out, cov_out = window_work(
        trans_map,
        process_noise,
        initial_expectation,
        steps_whole(map_rows),
        steps_whole(shift_rows),
        steps_whole(smooth_gains),
        steps_whole(filt_cov),
        lax.axis_index(CHUNKS),
        lax.axis_size(CHUNKS),
    )
    return (rows_of_steps(means_out), rows_of_steps(cov_out))


def solution(mesh):
    return jax.shard_map(
        per_device,
        mesh=mesh,
        in_specs=(
            P(),
            P(),
            P(),
            P(),
            P(),
            P(),
            P("tm", "blk", None),
            P("tm", None),
            P("tm", "blk", None),
            P("tm", "blk", None),
        ),
        out_specs=(P("tm", "blk"), P("tm", "blk", None)),
        check_vma=False,
    )
```

```python
import jax
import jax.numpy as jnp
from jax import lax
from jax.sharding import PartitionSpec as P

highest = lax.Precision.HIGHEST
CHUNKS = ("tm", "blk")


def from_behind(block, axis, distance):
    devices = range(lax.axis_size(axis))
    route = [(i - distance, i) for i in devices if i - distance in devices]
    return lax.ppermute(block, axis, route)


def expand_mask(mask, row_total, col_total):
    row_block = row_total // mask.shape[0]
    col_block = col_total // mask.shape[1]
    return jnp.repeat(jnp.repeat(mask.astype(jnp.float32), row_block, axis=0), col_block, axis=1)


def matmul(left, right):
    return jnp.matmul(left, right, precision=highest)


def matvec(left, right):
    return jnp.einsum("...ij,...j->...i", left, right, precision=highest)


def transpose(mats):
    return jnp.swapaxes(mats, -1, -2)


def filter_tree(maps, shifts):
    while maps.shape[0] > 1:
        early_map, late_map = maps[0::2], maps[1::2]
        shifts = matvec(late_map, shifts[0::2]) + shifts[1::2]
        maps = matmul(late_map, early_map)
    return maps[0], shifts[0]


def smooth_tree(gains, resids):
    levels = []
    while gains.shape[0] > 1:
        outer, inner = gains[0::2], gains[1::2]
        levels.append(outer)
        resids = matmul(matmul(outer, resids[1::2]), transpose(outer)) + resids[0::2]
        gains = matmul(outer, inner)
    return gains[0], resids[0], levels


def offset_tree(levels, offsets):
    for outer in levels:
        offsets = matvec(outer, offsets[1::2]) + offsets[0::2]
    return offsets[0]


def filter_scan(window_map, window_shift, initial_expectation, tm_index, tm_count):
    width = window_map.shape[0]
    first_window = tm_index == 0
    shift = jnp.where(first_window, matvec(window_map, initial_expectation) + window_shift, window_shift)
    cmap = jnp.where(first_window, jnp.float32(0.0), window_map)
    distance = 1
    while distance < tm_count:
        has_left = tm_index >= distance
        if 2 * distance >= tm_count:
            shift_left = from_behind(shift, CHUNKS, distance)
            shift = jnp.where(has_left, matvec(cmap, shift_left) + shift, shift)
        else:
            arrived = from_behind(jnp.concatenate([cmap, shift[None]], axis=0), CHUNKS, distance)
            map_left, shift_left = arrived[:width], arrived[width]
            shift = jnp.where(has_left, matvec(cmap, shift_left) + shift, shift)
            cmap = jnp.where(has_left, matmul(cmap, map_left), cmap)
        distance *= 2
    mean_in = from_behind(shift, CHUNKS, 1)
    return jnp.where(first_window, initial_expectation, mean_in)


def cov_scan(window_gain, window_resid, tm_index, tm_count):
    gain, resid = window_gain, window_resid
    round_gains = []
    distance = 1
    while distance < tm_count:
        has_right = tm_index + distance < tm_count
        round_gains.append(gain)
        if 2 * distance >= tm_count:
            resid_right = from_behind(resid, CHUNKS, -distance)
        else:
            arrived = from_behind(jnp.concatenate([gain, resid], axis=0), CHUNKS, -distance)
            gain_right, resid_right = jnp.split(arrived, 2, axis=0)
        new_resid = matmul(matmul(gain, resid_right), gain.T) + resid
        resid = jnp.where(has_right, new_resid, resid)
        if 2 * distance < tm_count:
            gain = jnp.where(has_right, matmul(gain, gain_right), gain)
        distance *= 2
    cov_after = from_behind(resid, CHUNKS, -1)
    return jnp.where(tm_index == tm_count - 1, jnp.float32(0.0), cov_after), round_gains


def offset_scan(window_offset, round_gains, tm_index, tm_count):
    offset = window_offset
    distance = 1
    for gain in round_gains:
        has_right = tm_index + distance < tm_count
        offset_right = from_behind(offset, CHUNKS, -distance)
        offset = jnp.where(has_right, matvec(gain, offset_right) + offset, offset)
        distance *= 2
    mean_after = from_behind(offset, CHUNKS, -1)
    return jnp.where(tm_index == tm_count - 1, jnp.float32(0.0), mean_after)


def window_work(
    trans_map,
    process_noise,
    initial_expectation,
    transition_operators,
    step_shifts,
    gain_full,
    cov_full,
    tm_index,
    tm_count,
):
    step_count = transition_operators.shape[0]
    final_step = jnp.logical_and(tm_index == tm_count - 1, jnp.arange(step_count) == step_count - 1)
    gain_full = jnp.where(final_step[:, None, None], jnp.float32(0.0), gain_full)

    predicted = matmul(matmul(trans_map, cov_full), trans_map.T) + jnp.diag(process_noise)
    gain_trans = jnp.swapaxes(gain_full, 1, 2)
    residual_cov = cov_full - matmul(matmul(gain_full, predicted), gain_trans)
    window_gain, window_resid, gain_levels = smooth_tree(gain_full, residual_cov)
    cov_after, round_gains = cov_scan(window_gain, window_resid, tm_index, tm_count)

    window_map, window_shift = filter_tree(transition_operators, step_shifts)
    mean_in = filter_scan(window_map, window_shift, initial_expectation, tm_index, tm_count)

    filt_steps = []
    current = mean_in
    for step in range(step_count):
        current = matvec(transition_operators[step], current) + step_shifts[step]
        filt_steps.append(current)
    filt_means = jnp.stack(filt_steps)
    moved_means = jnp.einsum("ij,tj->ti", trans_map, filt_means, precision=highest)
    offsets = filt_means - jnp.einsum("tij,tj->ti", gain_full, moved_means, precision=highest)
    mean_after = offset_scan(offset_tree(gain_levels, offsets), round_gains, tm_index, tm_count)

    cov_steps = [None] * step_count
    mean_steps = [None] * step_count
    cov_next, mean_next = cov_after, mean_after
    for step in reversed(range(step_count)):
        gain_now = gain_full[step]
        cov_next = matmul(matmul(gain_now, cov_next), gain_now.T) + residual_cov[step]
        mean_next = matvec(gain_now, mean_next) + offsets[step]
        cov_steps[step] = cov_next
        mean_steps[step] = mean_next
    return jnp.stack(mean_steps), jnp.stack(cov_steps)


def per_device(
    dynamics,
    dynamics_mask,
    obs_op,
    obs_mask,
    process_noise,
    initial_expectation,
    filter_gains,
    observations,
    smooth_gains,
    filt_cov,
):
    width = dynamics.shape[0]
    obs_width = obs_op.shape[0]
    row_count = filter_gains.shape[1]
    row_start = lax.axis_index("blk") * row_count
    trans_map = dynamics * expand_mask(dynamics_mask, width, width)
    obs_map = obs_op * expand_mask(obs_mask, obs_width, width)
    obs_dyn = matmul(obs_map, trans_map)
    own_rows = lax.dynamic_slice_in_dim(trans_map, row_start, row_count, 0)
    map_rows = own_rows[None] - matmul(filter_gains, obs_dyn)
    shift_rows = jnp.einsum("tro,to->tr", filter_gains, observations, precision=highest)
    def steps_whole(rows):
        return lax.all_to_all(rows, "blk", 0, 1, tiled=True)

    def rows_of_steps(whole):
        return lax.all_to_all(whole, "blk", 1, 0, tiled=True)

    means_out, cov_out = window_work(
        trans_map,
        process_noise,
        initial_expectation,
        steps_whole(map_rows),
        steps_whole(shift_rows),
        steps_whole(smooth_gains),
        steps_whole(filt_cov),
        lax.axis_index(CHUNKS),
        lax.axis_size(CHUNKS),
    )
    return (rows_of_steps(means_out), rows_of_steps(cov_out))


def solution(mesh):
    return jax.shard_map(
        per_device,
        mesh=mesh,
        in_specs=(
            P(),
            P(),
            P(),
            P(),
            P(),
            P(),
            P("tm", "blk", None),
            P("tm", None),
            P("tm", "blk", None),
            P("tm", "blk", None),
        ),
        out_specs=(P("tm", "blk"), P("tm", "blk", None)),
        check_vma=False,
    )
```

```python
import jax
import jax.numpy as jnp
from jax import lax
from jax.sharding import PartitionSpec as P

highest = lax.Precision.HIGHEST
CHUNKS = ("tm", "blk")


def from_behind(block, axis, distance):
    devices = range(lax.axis_size(axis))
    route = [(i - distance, i) for i in devices if i - distance in devices]
    return lax.ppermute(block, axis, route)


def expand_mask(mask, row_total, col_total):
    row_block = row_total // mask.shape[0]
    col_block = col_total // mask.shape[1]
    return jnp.repeat(jnp.repeat(mask.astype(jnp.float32), row_block, axis=0), col_block, axis=1)


def matmul(left, right):
    return jnp.matmul(left, right, precision=highest)


def matvec(left, right):
    return jnp.einsum("...ij,...j->...i", left, right, precision=highest)


def transpose(mats):
    return jnp.swapaxes(mats, -1, -2)


def filter_tree(maps, shifts):
    while maps.shape[0] > 1:
        early_map, late_map = maps[0::2], maps[1::2]
        shifts = matvec(late_map, shifts[0::2]) + shifts[1::2]
        maps = matmul(late_map, early_map)
    return maps[0], shifts[0]


def smooth_tree(gains, resids):
    levels = []
    while gains.shape[0] > 1:
        outer, inner = gains[0::2], gains[1::2]
        levels.append(outer)
        resids = matmul(matmul(outer, resids[1::2]), transpose(outer)) + resids[0::2]
        gains = matmul(outer, inner)
    return gains[0], resids[0], levels


def offset_tree(levels, offsets):
    for outer in levels:
        offsets = matvec(outer, offsets[1::2]) + offsets[0::2]
    return offsets[0]


def filter_scan(window_map, window_shift, initial_expectation, tm_index, tm_count):
    width = window_map.shape[0]
    first_window = tm_index == 0
    shift = jnp.where(first_window, matvec(window_map, initial_expectation) + window_shift, window_shift)
    cmap = jnp.where(first_window, jnp.float32(0.0), window_map)
    distance = 1
    while distance < tm_count:
        has_left = tm_index >= distance
        if 2 * distance >= tm_count:
            shift_left = from_behind(shift, CHUNKS, distance)
            shift = jnp.where(has_left, matvec(cmap, shift_left) + shift, shift)
        else:
            arrived = from_behind(jnp.concatenate([cmap, shift[None]], axis=0), CHUNKS, distance)
            map_left, shift_left = arrived[:width], arrived[width]
            shift = jnp.where(has_left, matvec(cmap, shift_left) + shift, shift)
            cmap = jnp.where(has_left, matmul(cmap, map_left), cmap)
        distance *= 2
    mean_in = from_behind(shift, CHUNKS, 1)
    return jnp.where(first_window, initial_expectation, mean_in)


def cov_scan(window_gain, window_resid, tm_index, tm_count):
    gain, resid = window_gain, window_resid
    round_gains = []
    distance = 1
    while distance < tm_count:
        has_right = tm_index + distance < tm_count
        round_gains.append(gain)
        if 2 * distance >= tm_count:
            resid_right = from_behind(resid, CHUNKS, -distance)
        else:
            arrived = from_behind(jnp.concatenate([gain, resid], axis=0), CHUNKS, -distance)
            gain_right, resid_right = jnp.split(arrived, 2, axis=0)
        new_resid = matmul(matmul(gain, resid_right), gain.T) + resid
        resid = jnp.where(has_right, new_resid, resid)
        if 2 * distance < tm_count:
            gain = jnp.where(has_right, matmul(gain, gain_right), gain)
        distance *= 2
    cov_after = from_behind(resid, CHUNKS, -1)
    return jnp.where(tm_index == tm_count - 1, jnp.float32(0.0), cov_after), round_gains


def offset_scan(window_offset, round_gains, tm_index, tm_count):
    offset = window_offset
    distance = 1
    for gain in round_gains:
        has_right = tm_index + distance < tm_count
        offset_right = from_behind(offset, CHUNKS, -distance)
        offset = jnp.where(has_right, matvec(gain, offset_right) + offset, offset)
        distance *= 2
    mean_after = from_behind(offset, CHUNKS, -1)
    return jnp.where(tm_index == tm_count - 1, jnp.float32(0.0), mean_after)


def window_work(
    trans_map,
    process_noise,
    initial_expectation,
    transition_operators,
    step_shifts,
    gain_full,
    cov_full,
    tm_index,
    tm_count,
):
    step_count = transition_operators.shape[0]
    final_step = jnp.logical_and(tm_index == tm_count - 1, jnp.arange(step_count) == step_count - 1)
    gain_full = jnp.where(final_step[:, None, None], jnp.float32(0.0), gain_full)

    predicted = matmul(matmul(trans_map, cov_full), trans_map.T) + jnp.diag(process_noise)
    gain_trans = jnp.swapaxes(gain_full, 1, 2)
    residual_cov = cov_full - matmul(matmul(gain_full, predicted), gain_trans)
    window_gain, window_resid, gain_levels = smooth_tree(gain_full, residual_cov)
    cov_after, round_gains = cov_scan(window_gain, window_resid, tm_index, tm_count)

    window_map, window_shift = filter_tree(transition_operators, step_shifts)
    mean_in = filter_scan(window_map, window_shift, initial_expectation, tm_index, tm_count)

    filt_steps = []
    current = mean_in
    for step in range(step_count):
        current = matvec(transition_operators[step], current) + step_shifts[step]
        filt_steps.append(current)
    filt_means = jnp.stack(filt_steps)
    moved_means = jnp.einsum("ij,tj->ti", trans_map, filt_means, precision=highest)
    offsets = filt_means - jnp.einsum("tij,tj->ti", gain_full, moved_means, precision=highest)
    mean_after = offset_scan(offset_tree(gain_levels, offsets), round_gains, tm_index, tm_count)

    cov_steps = [None] * step_count
    mean_steps = [None] * step_count
    cov_next, mean_next = cov_after, mean_after
    for step in reversed(range(step_count)):
        gain_now = gain_full[step]
        cov_next = matmul(matmul(gain_now, cov_next), gain_now.T) + residual_cov[step]
        mean_next = matvec(gain_now, mean_next) + offsets[step]
        cov_steps[step] = lax.all_to_all(cov_next[None], "blk", 1, 0, tiled=True)
        mean_steps[step] = mean_next
    cov_rows = jnp.stack(cov_steps, axis=1)
    cov_rows = cov_rows.reshape((-1,) + cov_rows.shape[2:])
    return jnp.stack(mean_steps), cov_rows


def per_device(
    dynamics,
    dynamics_mask,
    obs_op,
    obs_mask,
    process_noise,
    initial_expectation,
    filter_gains,
    observations,
    smooth_gains,
    filt_cov,
):
    width = dynamics.shape[0]
    obs_width = obs_op.shape[0]
    row_count = filter_gains.shape[1]
    row_start = lax.axis_index("blk") * row_count
    trans_map = dynamics * expand_mask(dynamics_mask, width, width)
    obs_map = obs_op * expand_mask(obs_mask, obs_width, width)
    obs_dyn = matmul(obs_map, trans_map)
    own_rows = lax.dynamic_slice_in_dim(trans_map, row_start, row_count, 0)
    map_rows = own_rows[None] - matmul(filter_gains, obs_dyn)
    shift_rows = jnp.einsum("tro,to->tr", filter_gains, observations, precision=highest)
    def steps_whole(rows):
        return lax.all_to_all(rows, "blk", 0, 1, tiled=True)

    gain_cov = steps_whole(jnp.concatenate([smooth_gains, filt_cov], axis=2))
    gain_whole, cov_whole = jnp.split(gain_cov, 2, axis=2)
    map_rows, shift_rows, gain_cov = lax.optimization_barrier((map_rows, shift_rows, gain_cov))

    means_out, cov_out = window_work(
        trans_map,
        process_noise,
        initial_expectation,
        steps_whole(map_rows),
        steps_whole(shift_rows),
        gain_whole,
        cov_whole,
        lax.axis_index(CHUNKS),
        lax.axis_size(CHUNKS),
    )
    return (lax.all_to_all(means_out, "blk", 1, 0, tiled=True), cov_out)


def solution(mesh):
    return jax.shard_map(
        per_device,
        mesh=mesh,
        in_specs=(
            P(),
            P(),
            P(),
            P(),
            P(),
            P(),
            P("tm", "blk", None),
            P("tm", None),
            P("tm", "blk", None),
            P("tm", "blk", None),
        ),
        out_specs=(P("tm", "blk"), P("tm", "blk", None)),
        check_vma=False,
    )
```

```python
import jax
import jax.numpy as jnp
from jax import lax
from jax.sharding import PartitionSpec as P

highest = lax.Precision.HIGHEST
CHUNKS = ("tm", "blk")


def from_behind(block, axis, distance):
    devices = range(lax.axis_size(axis))
    route = [(i - distance, i) for i in devices if i - distance in devices]
    return lax.ppermute(block, axis, route)


def expand_mask(mask, row_total, col_total):
    row_block = row_total // mask.shape[0]
    col_block = col_total // mask.shape[1]
    return jnp.repeat(jnp.repeat(mask.astype(jnp.float32), row_block, axis=0), col_block, axis=1)


def matmul(left, right):
    return jnp.matmul(left, right, precision=highest)


def matvec(left, right):
    return jnp.einsum("...ij,...j->...i", left, right, precision=highest)


def transpose(mats):
    return jnp.swapaxes(mats, -1, -2)


def filter_tree(maps, shifts):
    while maps.shape[0] > 1:
        early_map, late_map = maps[0::2], maps[1::2]
        shifts = matvec(late_map, shifts[0::2]) + shifts[1::2]
        maps = matmul(late_map, early_map)
    return maps[0], shifts[0]


def smooth_tree(gains, resids):
    levels = []
    while gains.shape[0] > 1:
        outer, inner = gains[0::2], gains[1::2]
        levels.append(outer)
        resids = matmul(matmul(outer, resids[1::2]), transpose(outer)) + resids[0::2]
        gains = matmul(outer, inner)
    return gains[0], resids[0], levels


def offset_tree(levels, offsets):
    for outer in levels:
        offsets = matvec(outer, offsets[1::2]) + offsets[0::2]
    return offsets[0]


def filter_scan(window_map, window_shift, initial_expectation, tm_index, tm_count):
    width = window_map.shape[0]
    first_window = tm_index == 0
    shift = jnp.where(first_window, matvec(window_map, initial_expectation) + window_shift, window_shift)
    cmap = jnp.where(first_window, jnp.float32(0.0), window_map)
    distance = 1
    while distance < tm_count:
        has_left = tm_index >= distance
        if 2 * distance >= tm_count:
            shift_left = from_behind(shift, CHUNKS, distance)
            shift = jnp.where(has_left, matvec(cmap, shift_left) + shift, shift)
        else:
            arrived = from_behind(jnp.concatenate([cmap, shift[None]], axis=0), CHUNKS, distance)
            map_left, shift_left = arrived[:width], arrived[width]
            shift = jnp.where(has_left, matvec(cmap, shift_left) + shift, shift)
            cmap = jnp.where(has_left, matmul(cmap, map_left), cmap)
        distance *= 2
    mean_in = from_behind(shift, CHUNKS, 1)
    return jnp.where(first_window, initial_expectation, mean_in)


def cov_scan(window_gain, window_resid, tm_index, tm_count):
    gain, resid = window_gain, window_resid
    round_gains = []
    distance = 1
    while 2 * distance < tm_count:
        has_right = tm_index + distance < tm_count
        round_gains.append(gain)
        arrived = from_behind(jnp.concatenate([gain, resid], axis=0), CHUNKS, -distance)
        gain_right, resid_right = jnp.split(arrived, 2, axis=0)
        new_resid = matmul(matmul(gain, resid_right), gain.T) + resid
        resid = jnp.where(has_right, new_resid, resid)
        gain = jnp.where(has_right, matmul(gain, gain_right), gain)
        distance *= 2
    round_gains.append(gain)
    gain_next, resid_next = jnp.split(
        from_behind(jnp.concatenate([gain, resid], axis=0), CHUNKS, -1), 2, axis=0
    )
    resid_far = from_behind(resid, CHUNKS, -(distance + 1))
    has_far = tm_index + distance + 1 < tm_count
    cov_after = jnp.where(
        has_far, matmul(matmul(gain_next, resid_far), gain_next.T) + resid_next, resid_next
    )
    return jnp.where(tm_index == tm_count - 1, jnp.float32(0.0), cov_after), round_gains


def offset_scan(window_offset, round_gains, tm_index, tm_count):
    offset = window_offset
    distance = 1
    for gain in round_gains:
        has_right = tm_index + distance < tm_count
        offset_right = from_behind(offset, CHUNKS, -distance)
        offset = jnp.where(has_right, matvec(gain, offset_right) + offset, offset)
        distance *= 2
    mean_after = from_behind(offset, CHUNKS, -1)
    return jnp.where(tm_index == tm_count - 1, jnp.float32(0.0), mean_after)


def window_work(
    trans_map,
    process_noise,
    initial_expectation,
    transition_operators,
    step_shifts,
    gain_full,
    cov_full,
    tm_index,
    tm_count,
):
    step_count = transition_operators.shape[0]
    final_step = jnp.logical_and(tm_index == tm_count - 1, jnp.arange(step_count) == step_count - 1)
    gain_full = jnp.where(final_step[:, None, None], jnp.float32(0.0), gain_full)

    predicted = matmul(matmul(trans_map, cov_full), trans_map.T) + jnp.diag(process_noise)
    gain_trans = jnp.swapaxes(gain_full, 1, 2)
    residual_cov = cov_full - matmul(matmul(gain_full, predicted), gain_trans)
    window_gain, window_resid, gain_levels = smooth_tree(gain_full, residual_cov)
    cov_after, round_gains = cov_scan(window_gain, window_resid, tm_index, tm_count)

    window_map, window_shift = filter_tree(transition_operators, step_shifts)
    mean_in = filter_scan(window_map, window_shift, initial_expectation, tm_index, tm_count)

    filt_steps = []
    current = mean_in
    for step in range(step_count):
        current = matvec(transition_operators[step], current) + step_shifts[step]
        filt_steps.append(current)
    filt_means = jnp.stack(filt_steps)
    moved_means = jnp.einsum("ij,tj->ti", trans_map, filt_means, precision=highest)
    offsets = filt_means - jnp.einsum("tij,tj->ti", gain_full, moved_means, precision=highest)
    mean_after = offset_scan(offset_tree(gain_levels, offsets), round_gains, tm_index, tm_count)

    cov_steps = [None] * step_count
    mean_steps = [None] * step_count
    cov_next, mean_next = cov_after, mean_after
    for step in reversed(range(step_count)):
        gain_now = gain_full[step]
        cov_next = matmul(matmul(gain_now, cov_next), gain_now.T) + residual_cov[step]
        mean_next = matvec(gain_now, mean_next) + offsets[step]
        cov_steps[step] = cov_next
        mean_steps[step] = mean_next
    return jnp.stack(mean_steps), jnp.stack(cov_steps)


def per_device(
    dynamics,
    dynamics_mask,
    obs_op,
    obs_mask,
    process_noise,
    initial_expectation,
    filter_gains,
    observations,
    smooth_gains,
    filt_cov,
):
    width = dynamics.shape[0]
    obs_width = obs_op.shape[0]
    row_count = filter_gains.shape[1]
    row_start = lax.axis_index("blk") * row_count
    trans_map = dynamics * expand_mask(dynamics_mask, width, width)
    obs_map = obs_op * expand_mask(obs_mask, obs_width, width)
    obs_dyn = matmul(obs_map, trans_map)
    own_rows = lax.dynamic_slice_in_dim(trans_map, row_start, row_count, 0)
    map_rows = own_rows[None] - matmul(filter_gains, obs_dyn)
    shift_rows = jnp.einsum("tro,to->tr", filter_gains, observations, precision=highest)
    def steps_whole(rows):
        return lax.all_to_all(rows, "blk", 0, 1, tiled=True)

    def rows_of_steps(whole):
        return lax.all_to_all(whole, "blk", 1, 0, tiled=True)

    means_out, cov_out = window_work(
        trans_map,
        process_noise,
        initial_expectation,
        steps_whole(map_rows),
        steps_whole(shift_rows),
        steps_whole(smooth_gains),
        steps_whole(filt_cov),
        lax.axis_index(CHUNKS),
        lax.axis_size(CHUNKS),
    )
    return (rows_of_steps(means_out), rows_of_steps(cov_out))


def solution(mesh):
    return jax.shard_map(
        per_device,
        mesh=mesh,
        in_specs=(
            P(),
            P(),
            P(),
            P(),
            P(),
            P(),
            P("tm", "blk", None),
            P("tm", None),
            P("tm", "blk", None),
            P("tm", "blk", None),
        ),
        out_specs=(P("tm", "blk"), P("tm", "blk", None)),
        check_vma=False,
    )
```

```python
import jax
import jax.numpy as jnp
from jax import lax
from jax.sharding import PartitionSpec as P

highest = lax.Precision.HIGHEST
CHUNKS = ("tm", "blk")


def from_behind(block, axis, distance):
    devices = range(lax.axis_size(axis))
    route = [(i - distance, i) for i in devices if i - distance in devices]
    return lax.ppermute(block, axis, route)


def expand_mask(mask, row_total, col_total):
    row_block = row_total // mask.shape[0]
    col_block = col_total // mask.shape[1]
    return jnp.repeat(jnp.repeat(mask.astype(jnp.float32), row_block, axis=0), col_block, axis=1)


def matmul(left, right):
    return jnp.matmul(left, right, precision=highest)


def matvec(left, right):
    return jnp.einsum("...ij,...j->...i", left, right, precision=highest)


def transpose(mats):
    return jnp.swapaxes(mats, -1, -2)


def filter_tree(maps, shifts):
    while maps.shape[0] > 1:
        early_map, late_map = maps[0::2], maps[1::2]
        shifts = matvec(late_map, shifts[0::2]) + shifts[1::2]
        maps = matmul(late_map, early_map)
    return maps[0], shifts[0]


def smooth_tree(gains, resids):
    levels = []
    while gains.shape[0] > 1:
        outer, inner = gains[0::2], gains[1::2]
        levels.append(outer)
        resids = matmul(matmul(outer, resids[1::2]), transpose(outer)) + resids[0::2]
        gains = matmul(outer, inner)
    return gains[0], resids[0], levels


def offset_tree(levels, offsets):
    for outer in levels:
        offsets = matvec(outer, offsets[1::2]) + offsets[0::2]
    return offsets[0]


def filter_scan(window_map, window_shift, initial_expectation, tm_index, tm_count):
    width = window_map.shape[0]
    first_window = tm_index == 0
    shift = jnp.where(first_window, matvec(window_map, initial_expectation) + window_shift, window_shift)
    cmap = jnp.where(first_window, jnp.float32(0.0), window_map)
    distance = 1
    while distance < tm_count:
        has_left = tm_index >= distance
        if 2 * distance >= tm_count:
            shift_left = from_behind(shift, CHUNKS, distance)
            shift = jnp.where(has_left, matvec(cmap, shift_left) + shift, shift)
        else:
            arrived = from_behind(jnp.concatenate([cmap, shift[None]], axis=0), CHUNKS, distance)
            map_left, shift_left = arrived[:width], arrived[width]
            shift = jnp.where(has_left, matvec(cmap, shift_left) + shift, shift)
            cmap = jnp.where(has_left, matmul(cmap, map_left), cmap)
        distance *= 2
    mean_in = from_behind(shift, CHUNKS, 1)
    return jnp.where(first_window, initial_expectation, mean_in)


def cov_rounds(gain, resid, tm_index, tm_count, stop):
    round_gains = []
    distance = 1
    while distance < stop and 2 * distance < tm_count:
        has_right = tm_index + distance < tm_count
        round_gains.append(gain)
        arrived = from_behind(jnp.concatenate([gain, resid], axis=0), CHUNKS, -distance)
        gain_right, resid_right = jnp.split(arrived, 2, axis=0)
        new_resid = matmul(matmul(gain, resid_right), gain.T) + resid
        resid = jnp.where(has_right, new_resid, resid)
        gain = jnp.where(has_right, matmul(gain, gain_right), gain)
        distance *= 2
    return gain, resid, round_gains, distance


def offset_rounds(offset, round_gains, tm_index, tm_count):
    distance = 1
    for gain in round_gains:
        has_right = tm_index + distance < tm_count
        offset_right = from_behind(offset, CHUNKS, -distance)
        offset = jnp.where(has_right, matvec(gain, offset_right) + offset, offset)
        distance *= 2
    return offset


def joint_rounds(gain, resid, offset, tm_index, tm_count, distance):
    width = gain.shape[0]
    while 2 * distance < tm_count:
        has_right = tm_index + distance < tm_count
        arrived = from_behind(
            jnp.concatenate([gain, resid, offset[None]], axis=0), CHUNKS, -distance
        )
        gain_right = arrived[:width]
        resid_right = arrived[width : 2 * width]
        offset_right = arrived[2 * width]
        new_resid = matmul(matmul(gain, resid_right), gain.T) + resid
        resid = jnp.where(has_right, new_resid, resid)
        offset = jnp.where(has_right, matvec(gain, offset_right) + offset, offset)
        gain = jnp.where(has_right, matmul(gain, gain_right), gain)
        distance *= 2
    arrived = from_behind(jnp.concatenate([gain, resid, offset[None]], axis=0), CHUNKS, -1)
    gain_next = arrived[:width]
    resid_next = arrived[width : 2 * width]
    offset_next = arrived[2 * width]
    far = from_behind(jnp.concatenate([resid, offset[None]], axis=0), CHUNKS, -(distance + 1))
    has_far = tm_index + distance + 1 < tm_count
    cov_after = jnp.where(
        has_far, matmul(matmul(gain_next, far[:width]), gain_next.T) + resid_next, resid_next
    )
    mean_after = jnp.where(has_far, matvec(gain_next, far[width]) + offset_next, offset_next)
    last_chunk = tm_index == tm_count - 1
    return (
        jnp.where(last_chunk, jnp.float32(0.0), cov_after),
        jnp.where(last_chunk, jnp.float32(0.0), mean_after),
    )


def window_work(
    trans_map,
    process_noise,
    initial_expectation,
    transition_operators,
    step_shifts,
    gain_full,
    cov_full,
    tm_index,
    tm_count,
):
    step_count = transition_operators.shape[0]
    final_step = jnp.logical_and(tm_index == tm_count - 1, jnp.arange(step_count) == step_count - 1)
    gain_full = jnp.where(final_step[:, None, None], jnp.float32(0.0), gain_full)

    predicted = matmul(matmul(trans_map, cov_full), trans_map.T) + jnp.diag(process_noise)
    gain_trans = jnp.swapaxes(gain_full, 1, 2)
    residual_cov = cov_full - matmul(matmul(gain_full, predicted), gain_trans)
    window_gain, window_resid, gain_levels = smooth_tree(gain_full, residual_cov)
    scan_gain, scan_resid, round_gains, distance = cov_rounds(
        window_gain, window_resid, tm_index, tm_count, 8
    )

    window_map, window_shift = filter_tree(transition_operators, step_shifts)
    mean_in = filter_scan(window_map, window_shift, initial_expectation, tm_index, tm_count)

    filt_steps = []
    current = mean_in
    for step in range(step_count):
        current = matvec(transition_operators[step], current) + step_shifts[step]
        filt_steps.append(current)
    filt_means = jnp.stack(filt_steps)
    moved_means = jnp.einsum("ij,tj->ti", trans_map, filt_means, precision=highest)
    offsets = filt_means - jnp.einsum("tij,tj->ti", gain_full, moved_means, precision=highest)
    scan_offset = offset_rounds(offset_tree(gain_levels, offsets), round_gains, tm_index, tm_count)
    cov_after, mean_after = joint_rounds(
        scan_gain, scan_resid, scan_offset, tm_index, tm_count, distance
    )

    cov_steps = [None] * step_count
    mean_steps = [None] * step_count
    cov_next, mean_next = cov_after, mean_after
    for step in reversed(range(step_count)):
        gain_now = gain_full[step]
        cov_next = matmul(matmul(gain_now, cov_next), gain_now.T) + residual_cov[step]
        mean_next = matvec(gain_now, mean_next) + offsets[step]
        cov_steps[step] = cov_next
        mean_steps[step] = mean_next
    return jnp.stack(mean_steps), jnp.stack(cov_steps)


def per_device(
    dynamics,
    dynamics_mask,
    obs_op,
    obs_mask,
    process_noise,
    initial_expectation,
    filter_gains,
    observations,
    smooth_gains,
    filt_cov,
):
    width = dynamics.shape[0]
    obs_width = obs_op.shape[0]
    row_count = filter_gains.shape[1]
    row_start = lax.axis_index("blk") * row_count
    trans_map = dynamics * expand_mask(dynamics_mask, width, width)
    obs_map = obs_op * expand_mask(obs_mask, obs_width, width)
    obs_dyn = matmul(obs_map, trans_map)
    own_rows = lax.dynamic_slice_in_dim(trans_map, row_start, row_count, 0)
    map_rows = own_rows[None] - matmul(filter_gains, obs_dyn)
    shift_rows = jnp.einsum("tro,to->tr", filter_gains, observations, precision=highest)
    def steps_whole(rows):
        return lax.all_to_all(rows, "blk", 0, 1, tiled=True)

    def rows_of_steps(whole):
        return lax.all_to_all(whole, "blk", 1, 0, tiled=True)

    means_out, cov_out = window_work(
        trans_map,
        process_noise,
        initial_expectation,
        steps_whole(map_rows),
        steps_whole(shift_rows),
        steps_whole(smooth_gains),
        steps_whole(filt_cov),
        lax.axis_index(CHUNKS),
        lax.axis_size(CHUNKS),
    )
    return (rows_of_steps(means_out), rows_of_steps(cov_out))


def solution(mesh):
    return jax.shard_map(
        per_device,
        mesh=mesh,
        in_specs=(
            P(),
            P(),
            P(),
            P(),
            P(),
            P(),
            P("tm", "blk", None),
            P("tm", None),
            P("tm", "blk", None),
            P("tm", "blk", None),
        ),
        out_specs=(P("tm", "blk"), P("tm", "blk", None)),
        check_vma=False,
    )
```

```python
import jax
import jax.numpy as jnp
from jax import lax
from jax.sharding import PartitionSpec as P

highest = lax.Precision.HIGHEST
CHUNKS = ("tm", "blk")


def from_behind(block, axis, distance):
    devices = range(lax.axis_size(axis))
    route = [(i - distance, i) for i in devices if i - distance in devices]
    return lax.ppermute(block, axis, route)


def expand_mask(mask, row_total, col_total):
    row_block = row_total // mask.shape[0]
    col_block = col_total // mask.shape[1]
    return jnp.repeat(jnp.repeat(mask.astype(jnp.float32), row_block, axis=0), col_block, axis=1)


def matmul(left, right):
    return jnp.matmul(left, right, precision=highest)


def matvec(left, right):
    return jnp.einsum("...ij,...j->...i", left, right, precision=highest)


def transpose(mats):
    return jnp.swapaxes(mats, -1, -2)


def filter_tree(maps, shifts):
    while maps.shape[0] > 1:
        early_map, late_map = maps[0::2], maps[1::2]
        shifts = matvec(late_map, shifts[0::2]) + shifts[1::2]
        maps = matmul(late_map, early_map)
    return maps[0], shifts[0]


def smooth_tree(gains, resids):
    levels = []
    while gains.shape[0] > 1:
        outer, inner = gains[0::2], gains[1::2]
        levels.append(outer)
        resids = matmul(matmul(outer, resids[1::2]), transpose(outer)) + resids[0::2]
        gains = matmul(outer, inner)
    return gains[0], resids[0], levels


def offset_tree(levels, offsets):
    for outer in levels:
        offsets = matvec(outer, offsets[1::2]) + offsets[0::2]
    return offsets[0]


def filter_scan(window_map, window_shift, initial_expectation, tm_index, tm_count):
    width = window_map.shape[0]
    first_window = tm_index == 0
    shift = jnp.where(first_window, matvec(window_map, initial_expectation) + window_shift, window_shift)
    cmap = jnp.where(first_window, jnp.float32(0.0), window_map)
    distance = 1
    while distance < tm_count:
        has_left = tm_index >= distance
        if 2 * distance >= tm_count:
            shift_left = from_behind(shift, CHUNKS, distance)
            shift = jnp.where(has_left, matvec(cmap, shift_left) + shift, shift)
        else:
            arrived = from_behind(jnp.concatenate([cmap, shift[None]], axis=0), CHUNKS, distance)
            map_left, shift_left = arrived[:width], arrived[width]
            shift = jnp.where(has_left, matvec(cmap, shift_left) + shift, shift)
            cmap = jnp.where(has_left, matmul(cmap, map_left), cmap)
        distance *= 2
    mean_in = from_behind(shift, CHUNKS, 1)
    return jnp.where(first_window, initial_expectation, mean_in)


def cov_scan(window_gain, window_resid, tm_index, tm_count):
    gain, resid = window_gain, window_resid
    round_gains = []
    distance = 1
    while distance < tm_count:
        has_right = tm_index + distance < tm_count
        round_gains.append(gain)
        if 2 * distance >= tm_count:
            resid_right = from_behind(resid, CHUNKS, -distance)
        else:
            arrived = from_behind(jnp.concatenate([gain, resid], axis=0), CHUNKS, -distance)
            gain_right, resid_right = jnp.split(arrived, 2, axis=0)
        new_resid = matmul(matmul(gain, resid_right), gain.T) + resid
        resid = jnp.where(has_right, new_resid, resid)
        if 2 * distance < tm_count:
            gain = jnp.where(has_right, matmul(gain, gain_right), gain)
        distance *= 2
    cov_after = from_behind(resid, CHUNKS, -1)
    return jnp.where(tm_index == tm_count - 1, jnp.float32(0.0), cov_after), round_gains


def offset_scan(window_offset, round_gains, tm_index, tm_count):
    offset = window_offset
    distance = 1
    for gain in round_gains:
        has_right = tm_index + distance < tm_count
        offset_right = from_behind(offset, CHUNKS, -distance)
        offset = jnp.where(has_right, matvec(gain, offset_right) + offset, offset)
        distance *= 2
    mean_after = from_behind(offset, CHUNKS, -1)
    return jnp.where(tm_index == tm_count - 1, jnp.float32(0.0), mean_after)


def window_work(
    trans_map,
    process_noise,
    initial_expectation,
    transition_operators,
    step_shifts,
    gain_full,
    cov_full,
    tm_index,
    tm_count,
):
    step_count = transition_operators.shape[0]
    final_step = jnp.logical_and(tm_index == tm_count - 1, jnp.arange(step_count) == step_count - 1)
    gain_full = jnp.where(final_step[:, None, None], jnp.float32(0.0), gain_full)

    predicted = matmul(matmul(trans_map, cov_full), trans_map.T) + jnp.diag(process_noise)
    gain_trans = jnp.swapaxes(gain_full, 1, 2)
    residual_cov = cov_full - matmul(matmul(gain_full, predicted), gain_trans)
    window_gain, window_resid, gain_levels = smooth_tree(gain_full, residual_cov)
    cov_after, round_gains = cov_scan(window_gain, window_resid, tm_index, tm_count)

    window_map, window_shift = filter_tree(transition_operators, step_shifts)
    mean_in = filter_scan(window_map, window_shift, initial_expectation, tm_index, tm_count)

    filt_steps = []
    current = mean_in
    for step in range(step_count):
        current = matvec(transition_operators[step], current) + step_shifts[step]
        filt_steps.append(current)
    filt_means = jnp.stack(filt_steps)
    moved_means = jnp.einsum("ij,tj->ti", trans_map, filt_means, precision=highest)
    offsets = filt_means - jnp.einsum("tij,tj->ti", gain_full, moved_means, precision=highest)
    mean_after = offset_scan(offset_tree(gain_levels, offsets), round_gains, tm_index, tm_count)

    cov_steps = [None] * step_count
    mean_steps = [None] * step_count
    cov_next, mean_next = cov_after, mean_after
    for step in reversed(range(step_count)):
        gain_now = gain_full[step]
        cov_next = matmul(matmul(gain_now, cov_next), gain_now.T) + residual_cov[step]
        mean_next = matvec(gain_now, mean_next) + offsets[step]
        cov_steps[step] = cov_next
        mean_steps[step] = mean_next
    return jnp.stack(mean_steps), jnp.stack(cov_steps)


def per_device(
    dynamics,
    dynamics_mask,
    obs_op,
    obs_mask,
    process_noise,
    initial_expectation,
    filter_gains,
    observations,
    smooth_gains,
    filt_cov,
):
    width = dynamics.shape[0]
    obs_width = obs_op.shape[0]
    row_count = filter_gains.shape[1]
    row_start = lax.axis_index("blk") * row_count
    trans_map = dynamics * expand_mask(dynamics_mask, width, width)
    obs_map = obs_op * expand_mask(obs_mask, obs_width, width)
    obs_dyn = matmul(obs_map, trans_map)
    own_rows = lax.dynamic_slice_in_dim(trans_map, row_start, row_count, 0)
    map_rows = own_rows[None] - matmul(filter_gains, obs_dyn)
    shift_rows = jnp.einsum("tro,to->tr", filter_gains, observations, precision=highest)
    blk_index = lax.axis_index("blk")
    blk_count = lax.axis_size("blk")

    def steps_whole(rows):
        blocks = rows.reshape((blk_count, rows.shape[0] // blk_count) + rows.shape[1:])
        pieces = []
        for shift in range(blk_count):
            block = lax.dynamic_index_in_dim(blocks, (blk_index + shift) % blk_count, 0, False)
            if shift > 0:
                route = [(j, (j + shift) % blk_count) for j in range(blk_count)]
                block = lax.ppermute(block, "blk", route)
            pieces.append(block)
        ordered = jnp.roll(jnp.stack(pieces[::-1]), blk_index + 1, axis=0)
        ordered = jnp.moveaxis(ordered, 0, 1)
        return ordered.reshape((ordered.shape[0], -1) + ordered.shape[3:])

    def rows_of_steps(whole):
        return lax.all_to_all(whole, "blk", 1, 0, tiled=True)

    means_out, cov_out = window_work(
        trans_map,
        process_noise,
        initial_expectation,
        steps_whole(map_rows),
        steps_whole(shift_rows),
        steps_whole(smooth_gains),
        steps_whole(filt_cov),
        lax.axis_index(CHUNKS),
        lax.axis_size(CHUNKS),
    )
    return (rows_of_steps(means_out), rows_of_steps(cov_out))


def solution(mesh):
    return jax.shard_map(
        per_device,
        mesh=mesh,
        in_specs=(
            P(),
            P(),
            P(),
            P(),
            P(),
            P(),
            P("tm", "blk", None),
            P("tm", None),
            P("tm", "blk", None),
            P("tm", "blk", None),
        ),
        out_specs=(P("tm", "blk"), P("tm", "blk", None)),
        check_vma=False,
    )
```

```python
import jax
import jax.numpy as jnp
from jax import lax
from jax.sharding import PartitionSpec as P

highest = lax.Precision.HIGHEST
CHUNKS = ("tm", "blk")


def from_behind(block, axis, distance):
    devices = range(lax.axis_size(axis))
    route = [(i - distance, i) for i in devices if i - distance in devices]
    return lax.ppermute(block, axis, route)


def expand_mask(mask, row_total, col_total):
    row_block = row_total // mask.shape[0]
    col_block = col_total // mask.shape[1]
    return jnp.repeat(jnp.repeat(mask.astype(jnp.float32), row_block, axis=0), col_block, axis=1)


def matmul(left, right):
    return jnp.matmul(left, right, precision=highest)


def matvec(left, right):
    return jnp.einsum("...ij,...j->...i", left, right, precision=highest)


def transpose(mats):
    return jnp.swapaxes(mats, -1, -2)


def filter_tree(maps, shifts):
    while maps.shape[0] > 1:
        early_map, late_map = maps[0::2], maps[1::2]
        shifts = matvec(late_map, shifts[0::2]) + shifts[1::2]
        maps = matmul(late_map, early_map)
    return maps[0], shifts[0]


def smooth_tree(gains, resids):
    levels = []
    while gains.shape[0] > 1:
        outer, inner = gains[0::2], gains[1::2]
        levels.append(outer)
        resids = matmul(matmul(outer, resids[1::2]), transpose(outer)) + resids[0::2]
        gains = matmul(outer, inner)
    return gains[0], resids[0], levels


def offset_tree(levels, offsets):
    for outer in levels:
        offsets = matvec(outer, offsets[1::2]) + offsets[0::2]
    return offsets[0]


def filter_scan(window_map, window_shift, initial_expectation, tm_index, tm_count):
    width = window_map.shape[0]
    first_window = tm_index == 0
    shift = jnp.where(first_window, matvec(window_map, initial_expectation) + window_shift, window_shift)
    cmap = jnp.where(first_window, jnp.float32(0.0), window_map)
    distance = 1
    while distance < tm_count:
        has_left = tm_index >= distance
        if 2 * distance >= tm_count:
            shift_left = from_behind(shift, CHUNKS, distance)
            shift = jnp.where(has_left, matvec(cmap, shift_left) + shift, shift)
        else:
            arrived = from_behind(jnp.concatenate([cmap, shift[None]], axis=0), CHUNKS, distance)
            map_left, shift_left = arrived[:width], arrived[width]
            shift = jnp.where(has_left, matvec(cmap, shift_left) + shift, shift)
            cmap = jnp.where(has_left, matmul(cmap, map_left), cmap)
        distance *= 2
    mean_in = from_behind(shift, CHUNKS, 1)
    return jnp.where(first_window, initial_expectation, mean_in)


def cov_scan(window_gain, window_resid, tm_index, tm_count):
    gain, resid = window_gain, window_resid
    round_gains = []
    distance = 1
    while distance < tm_count:
        has_right = tm_index + distance < tm_count
        round_gains.append(gain)
        if 2 * distance >= tm_count:
            resid_right = from_behind(resid, CHUNKS, -distance)
        else:
            arrived = from_behind(jnp.concatenate([gain, resid], axis=0), CHUNKS, -distance)
            gain_right, resid_right = jnp.split(arrived, 2, axis=0)
        new_resid = matmul(matmul(gain, resid_right), gain.T) + resid
        resid = jnp.where(has_right, new_resid, resid)
        if 2 * distance < tm_count:
            gain = jnp.where(has_right, matmul(gain, gain_right), gain)
        distance *= 2
    cov_after = from_behind(resid, CHUNKS, -1)
    return jnp.where(tm_index == tm_count - 1, jnp.float32(0.0), cov_after), round_gains


def offset_scan(window_offset, round_gains, tm_index, tm_count):
    offset = window_offset
    distance = 1
    for gain in round_gains:
        has_right = tm_index + distance < tm_count
        offset_right = from_behind(offset, CHUNKS, -distance)
        offset = jnp.where(has_right, matvec(gain, offset_right) + offset, offset)
        distance *= 2
    mean_after = from_behind(offset, CHUNKS, -1)
    return jnp.where(tm_index == tm_count - 1, jnp.float32(0.0), mean_after)


def window_work(
    trans_map,
    process_noise,
    initial_expectation,
    transition_operators,
    step_shifts,
    gain_full,
    cov_full,
    tm_index,
    tm_count,
):
    step_count = transition_operators.shape[0]
    final_step = jnp.logical_and(tm_index == tm_count - 1, jnp.arange(step_count) == step_count - 1)
    gain_full = jnp.where(final_step[:, None, None], jnp.float32(0.0), gain_full)

    predicted = matmul(matmul(trans_map, cov_full), trans_map.T) + jnp.diag(process_noise)
    gain_trans = jnp.swapaxes(gain_full, 1, 2)
    residual_cov = cov_full - matmul(matmul(gain_full, predicted), gain_trans)
    window_gain, window_resid, gain_levels = smooth_tree(gain_full, residual_cov)
    cov_after, round_gains = cov_scan(window_gain, window_resid, tm_index, tm_count)

    window_map, window_shift = filter_tree(transition_operators, step_shifts)
    mean_in = filter_scan(window_map, window_shift, initial_expectation, tm_index, tm_count)

    filt_steps = []
    current = mean_in
    for step in range(step_count):
        current = matvec(transition_operators[step], current) + step_shifts[step]
        filt_steps.append(current)
    filt_means = jnp.stack(filt_steps)
    moved_means = jnp.einsum("ij,tj->ti", trans_map, filt_means, precision=highest)
    offsets = filt_means - jnp.einsum("tij,tj->ti", gain_full, moved_means, precision=highest)
    mean_after = offset_scan(offset_tree(gain_levels, offsets), round_gains, tm_index, tm_count)

    cov_steps = [None] * step_count
    mean_steps = [None] * step_count
    cov_next, mean_next = cov_after, mean_after
    for step in reversed(range(step_count)):
        gain_now = gain_full[step]
        cov_next = matmul(matmul(gain_now, cov_next), gain_now.T) + residual_cov[step]
        mean_next = matvec(gain_now, mean_next) + offsets[step]
        cov_steps[step] = cov_next
        mean_steps[step] = mean_next
    return jnp.stack(mean_steps), jnp.stack(cov_steps)


def per_device(
    dynamics,
    dynamics_mask,
    obs_op,
    obs_mask,
    process_noise,
    initial_expectation,
    filter_gains,
    observations,
    smooth_gains,
    filt_cov,
):
    width = dynamics.shape[0]
    obs_width = obs_op.shape[0]
    row_count = filter_gains.shape[1]
    row_start = lax.axis_index("blk") * row_count
    trans_map = dynamics * expand_mask(dynamics_mask, width, width)
    obs_map = obs_op * expand_mask(obs_mask, obs_width, width)
    obs_dyn = matmul(obs_map, trans_map)
    own_rows = lax.dynamic_slice_in_dim(trans_map, row_start, row_count, 0)
    map_rows = own_rows[None] - matmul(filter_gains, obs_dyn)
    shift_rows = jnp.einsum("tro,to->tr", filter_gains, observations, precision=highest)
    def steps_whole(rows):
        return lax.all_to_all(rows, "blk", 0, 1, tiled=True)

    def rows_of_steps(whole):
        return lax.all_to_all(whole, "blk", 1, 0, tiled=True)

    gain_whole = steps_whole(smooth_gains)
    cov_whole = steps_whole(filt_cov)
    map_rows, shift_rows, gain_whole, cov_whole = lax.optimization_barrier(
        (map_rows, shift_rows, gain_whole, cov_whole)
    )
    means_out, cov_out = window_work(
        trans_map,
        process_noise,
        initial_expectation,
        steps_whole(map_rows),
        steps_whole(shift_rows),
        gain_whole,
        cov_whole,
        lax.axis_index(CHUNKS),
        lax.axis_size(CHUNKS),
    )
    return (rows_of_steps(means_out), rows_of_steps(cov_out))


def solution(mesh):
    return jax.shard_map(
        per_device,
        mesh=mesh,
        in_specs=(
            P(),
            P(),
            P(),
            P(),
            P(),
            P(),
            P("tm", "blk", None),
            P("tm", None),
            P("tm", "blk", None),
            P("tm", "blk", None),
        ),
        out_specs=(P("tm", "blk"), P("tm", "blk", None)),
        check_vma=False,
    )
```

```python
import jax
import jax.numpy as jnp
from jax import lax
from jax.sharding import PartitionSpec as P

highest = lax.Precision.HIGHEST
CHUNKS = ("tm", "blk")


def from_behind(block, axis, distance):
    devices = range(lax.axis_size(axis))
    route = [(i - distance, i) for i in devices if i - distance in devices]
    return lax.ppermute(block, axis, route)


def expand_mask(mask, row_total, col_total):
    row_block = row_total // mask.shape[0]
    col_block = col_total // mask.shape[1]
    return jnp.repeat(jnp.repeat(mask.astype(jnp.float32), row_block, axis=0), col_block, axis=1)


def matmul(left, right):
    return jnp.matmul(left, right, precision=highest)


def matvec(left, right):
    return jnp.einsum("...ij,...j->...i", left, right, precision=highest)


def transpose(mats):
    return jnp.swapaxes(mats, -1, -2)


def filter_tree(maps, shifts):
    while maps.shape[0] > 1:
        early_map, late_map = maps[0::2], maps[1::2]
        shifts = matvec(late_map, shifts[0::2]) + shifts[1::2]
        maps = matmul(late_map, early_map)
    return maps[0], shifts[0]


def smooth_tree(gains, resids):
    levels = []
    while gains.shape[0] > 1:
        outer, inner = gains[0::2], gains[1::2]
        levels.append(outer)
        resids = matmul(matmul(outer, resids[1::2]), transpose(outer)) + resids[0::2]
        gains = matmul(outer, inner)
    return gains[0], resids[0], levels


def offset_tree(levels, offsets):
    for outer in levels:
        offsets = matvec(outer, offsets[1::2]) + offsets[0::2]
    return offsets[0]


def filter_scan(window_map, window_shift, initial_expectation, tm_index, tm_count):
    width = window_map.shape[0]
    first_window = tm_index == 0
    shift = jnp.where(first_window, matvec(window_map, initial_expectation) + window_shift, window_shift)
    cmap = jnp.where(first_window, jnp.float32(0.0), window_map)
    distance = 1
    while distance < tm_count:
        has_left = tm_index >= distance
        if 2 * distance >= tm_count:
            shift_left = from_behind(shift, CHUNKS, distance)
            shift = jnp.where(has_left, matvec(cmap, shift_left) + shift, shift)
        else:
            arrived = from_behind(jnp.concatenate([cmap, shift[None]], axis=0), CHUNKS, distance)
            map_left, shift_left = arrived[:width], arrived[width]
            shift = jnp.where(has_left, matvec(cmap, shift_left) + shift, shift)
            cmap = jnp.where(has_left, matmul(cmap, map_left), cmap)
        distance *= 2
    mean_in = from_behind(shift, CHUNKS, 1)
    return jnp.where(first_window, initial_expectation, mean_in)


def tm_from(block, distance):
    count = lax.axis_size("tm")
    route = [(i + distance, i) for i in range(count) if 0 <= i + distance < count]
    return lax.ppermute(block, "tm", route)


def blk_gather(block):
    blk_index = lax.axis_index("blk")
    blk_count = lax.axis_size("blk")
    pieces = [block]
    for shift in range(1, blk_count):
        route = [(j, (j + shift) % blk_count) for j in range(blk_count)]
        pieces.append(lax.ppermute(block, "blk", route))
    return jnp.roll(jnp.stack(pieces[::-1]), blk_index + 1, axis=0)


def shared_from(pair, distance):
    blk_count = lax.axis_size("blk")
    rows = pair.shape[1] // blk_count
    part = lax.dynamic_slice_in_dim(pair, lax.axis_index("blk") * rows, rows, axis=1)
    gathered = blk_gather(tm_from(part, distance))
    gathered = jnp.moveaxis(gathered, 0, 1)
    return gathered.reshape(pair.shape)


def window_suffixes(chunk_gain, chunk_resid):
    width = chunk_gain.shape[0]
    gathered = blk_gather(jnp.stack([chunk_gain, chunk_resid]))
    blk_count = gathered.shape[0]
    gain, resid = gathered[blk_count - 1, 0], gathered[blk_count - 1, 1]
    gains = [jnp.eye(width, dtype=jnp.float32), gain]
    resids = [jnp.zeros((width, width), jnp.float32), resid]
    for j in reversed(range(blk_count - 1)):
        resid = matmul(matmul(gathered[j, 0], resid), gathered[j, 0].T) + gathered[j, 1]
        gain = matmul(gathered[j, 0], gain)
        gains.append(gain)
        resids.append(resid)
    return jnp.stack(gains[::-1]), jnp.stack(resids[::-1]), gathered[:, 0]


def offset_suffixes(chunk_offset, chunk_gains):
    gathered = blk_gather(chunk_offset)
    blk_count = gathered.shape[0]
    offset = gathered[blk_count - 1]
    offsets = [jnp.zeros_like(offset), offset]
    for j in reversed(range(blk_count - 1)):
        offset = matvec(chunk_gains[j], offset) + gathered[j]
        offsets.append(offset)
    return jnp.stack(offsets[::-1])


def window_cov_scan(gain, resid, tm_index, tm_count):
    round_gains = []
    distance = 1
    while distance < tm_count:
        has_right = tm_index + distance < tm_count
        round_gains.append(gain)
        if 2 * distance >= tm_count:
            resid_right = shared_from(resid[None], distance)[0]
        else:
            gain_right, resid_right = shared_from(jnp.stack([gain, resid]), distance)
        new_resid = matmul(matmul(gain, resid_right), gain.T) + resid
        resid = jnp.where(has_right, new_resid, resid)
        if 2 * distance < tm_count:
            gain = jnp.where(has_right, matmul(gain, gain_right), gain)
        distance *= 2
    cov_next = shared_from(resid[None], 1)[0]
    return jnp.where(tm_index == tm_count - 1, jnp.float32(0.0), cov_next), round_gains


def window_offset_scan(offset, round_gains, tm_index, tm_count):
    distance = 1
    for gain in round_gains:
        has_right = tm_index + distance < tm_count
        offset = jnp.where(has_right, matvec(gain, tm_from(offset, distance)) + offset, offset)
        distance *= 2
    mean_next = tm_from(offset, 1)
    return jnp.where(tm_index == tm_count - 1, jnp.float32(0.0), mean_next)


def window_work(
    trans_map,
    process_noise,
    initial_expectation,
    transition_operators,
    step_shifts,
    gain_full,
    cov_full,
    tm_index,
    tm_count,
):
    step_count = transition_operators.shape[0]
    final_step = jnp.logical_and(tm_index == tm_count - 1, jnp.arange(step_count) == step_count - 1)
    gain_full = jnp.where(final_step[:, None, None], jnp.float32(0.0), gain_full)

    predicted = matmul(matmul(trans_map, cov_full), trans_map.T) + jnp.diag(process_noise)
    gain_trans = jnp.swapaxes(gain_full, 1, 2)
    residual_cov = cov_full - matmul(matmul(gain_full, predicted), gain_trans)
    window_gain, window_resid, gain_levels = smooth_tree(gain_full, residual_cov)
    blk_index = lax.axis_index("blk")
    window_index = lax.axis_index("tm")
    window_count = lax.axis_size("tm")
    suffix_gains, suffix_resids, chunk_gains = window_suffixes(window_gain, window_resid)
    cov_next, round_gains = window_cov_scan(
        suffix_gains[0], suffix_resids[0], window_index, window_count
    )
    after_gain = lax.dynamic_index_in_dim(suffix_gains, blk_index + 1, 0, False)
    after_resid = lax.dynamic_index_in_dim(suffix_resids, blk_index + 1, 0, False)
    cov_after = matmul(matmul(after_gain, cov_next), after_gain.T) + after_resid

    window_map, window_shift = filter_tree(transition_operators, step_shifts)
    mean_in = filter_scan(window_map, window_shift, initial_expectation, tm_index, tm_count)

    filt_steps = []
    current = mean_in
    for step in range(step_count):
        current = matvec(transition_operators[step], current) + step_shifts[step]
        filt_steps.append(current)
    filt_means = jnp.stack(filt_steps)
    moved_means = jnp.einsum("ij,tj->ti", trans_map, filt_means, precision=highest)
    offsets = filt_means - jnp.einsum("tij,tj->ti", gain_full, moved_means, precision=highest)
    suffix_offsets = offset_suffixes(offset_tree(gain_levels, offsets), chunk_gains)
    mean_next = window_offset_scan(suffix_offsets[0], round_gains, window_index, window_count)
    after_offset = lax.dynamic_index_in_dim(suffix_offsets, blk_index + 1, 0, False)
    mean_after = matvec(after_gain, mean_next) + after_offset

    cov_steps = [None] * step_count
    mean_steps = [None] * step_count
    cov_next, mean_next = cov_after, mean_after
    for step in reversed(range(step_count)):
        gain_now = gain_full[step]
        cov_next = matmul(matmul(gain_now, cov_next), gain_now.T) + residual_cov[step]
        mean_next = matvec(gain_now, mean_next) + offsets[step]
        cov_steps[step] = cov_next
        mean_steps[step] = mean_next
    return jnp.stack(mean_steps), jnp.stack(cov_steps)


def per_device(
    dynamics,
    dynamics_mask,
    obs_op,
    obs_mask,
    process_noise,
    initial_expectation,
    filter_gains,
    observations,
    smooth_gains,
    filt_cov,
):
    width = dynamics.shape[0]
    obs_width = obs_op.shape[0]
    row_count = filter_gains.shape[1]
    row_start = lax.axis_index("blk") * row_count
    trans_map = dynamics * expand_mask(dynamics_mask, width, width)
    obs_map = obs_op * expand_mask(obs_mask, obs_width, width)
    obs_dyn = matmul(obs_map, trans_map)
    own_rows = lax.dynamic_slice_in_dim(trans_map, row_start, row_count, 0)
    map_rows = own_rows[None] - matmul(filter_gains, obs_dyn)
    shift_rows = jnp.einsum("tro,to->tr", filter_gains, observations, precision=highest)
    def steps_whole(rows):
        return lax.all_to_all(rows, "blk", 0, 1, tiled=True)

    def rows_of_steps(whole):
        return lax.all_to_all(whole, "blk", 1, 0, tiled=True)

    means_out, cov_out = window_work(
        trans_map,
        process_noise,
        initial_expectation,
        steps_whole(map_rows),
        steps_whole(shift_rows),
        steps_whole(smooth_gains),
        steps_whole(filt_cov),
        lax.axis_index(CHUNKS),
        lax.axis_size(CHUNKS),
    )
    return (rows_of_steps(means_out), rows_of_steps(cov_out))


def solution(mesh):
    return jax.shard_map(
        per_device,
        mesh=mesh,
        in_specs=(
            P(),
            P(),
            P(),
            P(),
            P(),
            P(),
            P("tm", "blk", None),
            P("tm", None),
            P("tm", "blk", None),
            P("tm", "blk", None),
        ),
        out_specs=(P("tm", "blk"), P("tm", "blk", None)),
        check_vma=False,
    )
```

```python
import jax
import jax.numpy as jnp
from jax import lax
from jax.sharding import PartitionSpec as P

highest = lax.Precision.HIGHEST
CHUNKS = ("tm", "blk")


def from_behind(block, axis, distance):
    devices = range(lax.axis_size(axis))
    route = [(i - distance, i) for i in devices if i - distance in devices]
    return lax.ppermute(block, axis, route)


def expand_mask(mask, row_total, col_total):
    row_block = row_total // mask.shape[0]
    col_block = col_total // mask.shape[1]
    return jnp.repeat(jnp.repeat(mask.astype(jnp.float32), row_block, axis=0), col_block, axis=1)


def matmul(left, right):
    return jnp.matmul(left, right, precision=highest)


def matvec(left, right):
    return jnp.einsum("...ij,...j->...i", left, right, precision=highest)


def transpose(mats):
    return jnp.swapaxes(mats, -1, -2)


def filter_tree(maps, shifts):
    while maps.shape[0] > 1:
        early_map, late_map = maps[0::2], maps[1::2]
        shifts = matvec(late_map, shifts[0::2]) + shifts[1::2]
        maps = matmul(late_map, early_map)
    return maps[0], shifts[0]


def smooth_tree(gains, resids):
    levels = []
    while gains.shape[0] > 1:
        outer, inner = gains[0::2], gains[1::2]
        levels.append(outer)
        resids = matmul(matmul(outer, resids[1::2]), transpose(outer)) + resids[0::2]
        gains = matmul(outer, inner)
    return gains[0], resids[0], levels


def offset_tree(levels, offsets):
    for outer in levels:
        offsets = matvec(outer, offsets[1::2]) + offsets[0::2]
    return offsets[0]


def filter_scan(window_map, window_shift, initial_expectation, tm_index, tm_count):
    width = window_map.shape[0]
    first_window = tm_index == 0
    shift = jnp.where(first_window, matvec(window_map, initial_expectation) + window_shift, window_shift)
    cmap = jnp.where(first_window, jnp.float32(0.0), window_map)
    distance = 1
    while distance < tm_count:
        has_left = tm_index >= distance
        if 2 * distance >= tm_count:
            shift_left = from_behind(shift, CHUNKS, distance)
            shift = jnp.where(has_left, matvec(cmap, shift_left) + shift, shift)
        else:
            arrived = from_behind(jnp.concatenate([cmap, shift[None]], axis=0), CHUNKS, distance)
            map_left, shift_left = arrived[:width], arrived[width]
            shift = jnp.where(has_left, matvec(cmap, shift_left) + shift, shift)
            cmap = jnp.where(has_left, matmul(cmap, map_left), cmap)
        distance *= 2
    mean_in = from_behind(shift, CHUNKS, 1)
    return jnp.where(first_window, initial_expectation, mean_in)


def cov_scan(window_gain, window_resid, tm_index, tm_count):
    gain, resid = window_gain, window_resid
    round_gains = []
    distance = 1
    while distance < tm_count:
        has_right = tm_index + distance < tm_count
        round_gains.append(gain)
        resid_right = from_behind(resid, CHUNKS, -distance)
        if 2 * distance < tm_count:
            gain_right = from_behind(gain, CHUNKS, -distance)
        new_resid = matmul(matmul(gain, resid_right), gain.T) + resid
        resid = jnp.where(has_right, new_resid, resid)
        if 2 * distance < tm_count:
            gain = jnp.where(has_right, matmul(gain, gain_right), gain)
        distance *= 2
    cov_after = from_behind(resid, CHUNKS, -1)
    return jnp.where(tm_index == tm_count - 1, jnp.float32(0.0), cov_after), round_gains


def offset_scan(window_offset, round_gains, tm_index, tm_count):
    offset = window_offset
    distance = 1
    for gain in round_gains:
        has_right = tm_index + distance < tm_count
        offset_right = from_behind(offset, CHUNKS, -distance)
        offset = jnp.where(has_right, matvec(gain, offset_right) + offset, offset)
        distance *= 2
    mean_after = from_behind(offset, CHUNKS, -1)
    return jnp.where(tm_index == tm_count - 1, jnp.float32(0.0), mean_after)


def window_work(
    trans_map,
    process_noise,
    initial_expectation,
    transition_operators,
    step_shifts,
    gain_full,
    cov_full,
    tm_index,
    tm_count,
):
    step_count = transition_operators.shape[0]
    final_step = jnp.logical_and(tm_index == tm_count - 1, jnp.arange(step_count) == step_count - 1)
    gain_full = jnp.where(final_step[:, None, None], jnp.float32(0.0), gain_full)

    predicted = matmul(matmul(trans_map, cov_full), trans_map.T) + jnp.diag(process_noise)
    gain_trans = jnp.swapaxes(gain_full, 1, 2)
    residual_cov = cov_full - matmul(matmul(gain_full, predicted), gain_trans)
    window_gain, window_resid, gain_levels = smooth_tree(gain_full, residual_cov)
    cov_after, round_gains = cov_scan(window_gain, window_resid, tm_index, tm_count)

    window_map, window_shift = filter_tree(transition_operators, step_shifts)
    mean_in = filter_scan(window_map, window_shift, initial_expectation, tm_index, tm_count)

    filt_steps = []
    current = mean_in
    for step in range(step_count):
        current = matvec(transition_operators[step], current) + step_shifts[step]
        filt_steps.append(current)
    filt_means = jnp.stack(filt_steps)
    moved_means = jnp.einsum("ij,tj->ti", trans_map, filt_means, precision=highest)
    offsets = filt_means - jnp.einsum("tij,tj->ti", gain_full, moved_means, precision=highest)
    mean_after = offset_scan(offset_tree(gain_levels, offsets), round_gains, tm_index, tm_count)

    cov_steps = [None] * step_count
    mean_steps = [None] * step_count
    cov_next, mean_next = cov_after, mean_after
    for step in reversed(range(step_count)):
        gain_now = gain_full[step]
        cov_next = matmul(matmul(gain_now, cov_next), gain_now.T) + residual_cov[step]
        mean_next = matvec(gain_now, mean_next) + offsets[step]
        cov_steps[step] = cov_next
        mean_steps[step] = mean_next
    return jnp.stack(mean_steps), jnp.stack(cov_steps)


def per_device(
    dynamics,
    dynamics_mask,
    obs_op,
    obs_mask,
    process_noise,
    initial_expectation,
    filter_gains,
    observations,
    smooth_gains,
    filt_cov,
):
    width = dynamics.shape[0]
    obs_width = obs_op.shape[0]
    row_count = filter_gains.shape[1]
    row_start = lax.axis_index("blk") * row_count
    trans_map = dynamics * expand_mask(dynamics_mask, width, width)
    obs_map = obs_op * expand_mask(obs_mask, obs_width, width)
    obs_dyn = matmul(obs_map, trans_map)
    own_rows = lax.dynamic_slice_in_dim(trans_map, row_start, row_count, 0)
    map_rows = own_rows[None] - matmul(filter_gains, obs_dyn)
    shift_rows = jnp.einsum("tro,to->tr", filter_gains, observations, precision=highest)
    def steps_whole(rows):
        return lax.all_to_all(rows, "blk", 0, 1, tiled=True)

    def rows_of_steps(whole):
        return lax.all_to_all(whole, "blk", 1, 0, tiled=True)

    means_out, cov_out = window_work(
        trans_map,
        process_noise,
        initial_expectation,
        steps_whole(map_rows),
        steps_whole(shift_rows),
        steps_whole(smooth_gains),
        steps_whole(filt_cov),
        lax.axis_index(CHUNKS),
        lax.axis_size(CHUNKS),
    )
    return (rows_of_steps(means_out), rows_of_steps(cov_out))


def solution(mesh):
    return jax.shard_map(
        per_device,
        mesh=mesh,
        in_specs=(
            P(),
            P(),
            P(),
            P(),
            P(),
            P(),
            P("tm", "blk", None),
            P("tm", None),
            P("tm", "blk", None),
            P("tm", "blk", None),
        ),
        out_specs=(P("tm", "blk"), P("tm", "blk", None)),
        check_vma=False,
    )
```

```python
import jax
import jax.numpy as jnp
from jax import lax
from jax.sharding import PartitionSpec as P

highest = lax.Precision.HIGHEST
CHUNKS = ("tm", "blk")


def from_behind(block, axis, distance):
    devices = range(lax.axis_size(axis))
    route = [(i - distance, i) for i in devices if i - distance in devices]
    return lax.ppermute(block, axis, route)


def expand_mask(mask, row_total, col_total):
    row_block = row_total // mask.shape[0]
    col_block = col_total // mask.shape[1]
    return jnp.repeat(jnp.repeat(mask.astype(jnp.float32), row_block, axis=0), col_block, axis=1)


def matmul(left, right):
    return jnp.matmul(left, right, precision=highest)


def matvec(left, right):
    return jnp.einsum("...ij,...j->...i", left, right, precision=highest)


def transpose(mats):
    return jnp.swapaxes(mats, -1, -2)


def filter_tree(maps, shifts):
    while maps.shape[0] > 1:
        early_map, late_map = maps[0::2], maps[1::2]
        shifts = matvec(late_map, shifts[0::2]) + shifts[1::2]
        maps = matmul(late_map, early_map)
    return maps[0], shifts[0]


def smooth_tree(gains, resids):
    levels = []
    while gains.shape[0] > 1:
        outer, inner = gains[0::2], gains[1::2]
        levels.append(outer)
        resids = matmul(matmul(outer, resids[1::2]), transpose(outer)) + resids[0::2]
        gains = matmul(outer, inner)
    return gains[0], resids[0], levels


def offset_tree(levels, offsets):
    for outer in levels:
        offsets = matvec(outer, offsets[1::2]) + offsets[0::2]
    return offsets[0]


def filter_scan(window_map, window_shift, initial_expectation, tm_index, tm_count):
    width = window_map.shape[0]
    first_window = tm_index == 0
    shift = jnp.where(first_window, matvec(window_map, initial_expectation) + window_shift, window_shift)
    cmap = jnp.where(first_window, jnp.float32(0.0), window_map)
    distance = 1
    while distance < tm_count:
        has_left = tm_index >= distance
        if 2 * distance >= tm_count:
            shift_left = from_behind(shift, CHUNKS, distance)
            shift = jnp.where(has_left, matvec(cmap, shift_left) + shift, shift)
        else:
            shift_left = from_behind(shift, CHUNKS, distance)
            map_left = from_behind(cmap, CHUNKS, distance)
            shift = jnp.where(has_left, matvec(cmap, shift_left) + shift, shift)
            cmap = jnp.where(has_left, matmul(cmap, map_left), cmap)
        distance *= 2
    mean_in = from_behind(shift, CHUNKS, 1)
    return jnp.where(first_window, initial_expectation, mean_in)


def cov_scan(window_gain, window_resid, tm_index, tm_count):
    gain, resid = window_gain, window_resid
    round_gains = []
    distance = 1
    while distance < tm_count:
        has_right = tm_index + distance < tm_count
        round_gains.append(gain)
        resid_right = from_behind(resid, CHUNKS, -distance)
        if 2 * distance < tm_count:
            gain_right = from_behind(gain, CHUNKS, -distance)
        new_resid = matmul(matmul(gain, resid_right), gain.T) + resid
        resid = jnp.where(has_right, new_resid, resid)
        if 2 * distance < tm_count:
            gain = jnp.where(has_right, matmul(gain, gain_right), gain)
        distance *= 2
    cov_after = from_behind(resid, CHUNKS, -1)
    return jnp.where(tm_index == tm_count - 1, jnp.float32(0.0), cov_after), round_gains


def offset_scan(window_offset, round_gains, tm_index, tm_count):
    offset = window_offset
    distance = 1
    for gain in round_gains:
        has_right = tm_index + distance < tm_count
        offset_right = from_behind(offset, CHUNKS, -distance)
        offset = jnp.where(has_right, matvec(gain, offset_right) + offset, offset)
        distance *= 2
    mean_after = from_behind(offset, CHUNKS, -1)
    return jnp.where(tm_index == tm_count - 1, jnp.float32(0.0), mean_after)


def window_work(
    trans_map,
    process_noise,
    initial_expectation,
    transition_operators,
    step_shifts,
    gain_full,
    cov_full,
    tm_index,
    tm_count,
):
    step_count = transition_operators.shape[0]
    final_step = jnp.logical_and(tm_index == tm_count - 1, jnp.arange(step_count) == step_count - 1)
    gain_full = jnp.where(final_step[:, None, None], jnp.float32(0.0), gain_full)

    predicted = matmul(matmul(trans_map, cov_full), trans_map.T) + jnp.diag(process_noise)
    gain_trans = jnp.swapaxes(gain_full, 1, 2)
    residual_cov = cov_full - matmul(matmul(gain_full, predicted), gain_trans)
    window_gain, window_resid, gain_levels = smooth_tree(gain_full, residual_cov)
    cov_after, round_gains = cov_scan(window_gain, window_resid, tm_index, tm_count)

    window_map, window_shift = filter_tree(transition_operators, step_shifts)
    mean_in = filter_scan(window_map, window_shift, initial_expectation, tm_index, tm_count)

    filt_steps = []
    current = mean_in
    for step in range(step_count):
        current = matvec(transition_operators[step], current) + step_shifts[step]
        filt_steps.append(current)
    filt_means = jnp.stack(filt_steps)
    moved_means = jnp.einsum("ij,tj->ti", trans_map, filt_means, precision=highest)
    offsets = filt_means - jnp.einsum("tij,tj->ti", gain_full, moved_means, precision=highest)
    mean_after = offset_scan(offset_tree(gain_levels, offsets), round_gains, tm_index, tm_count)

    cov_steps = [None] * step_count
    mean_steps = [None] * step_count
    cov_next, mean_next = cov_after, mean_after
    for step in reversed(range(step_count)):
        gain_now = gain_full[step]
        cov_next = matmul(matmul(gain_now, cov_next), gain_now.T) + residual_cov[step]
        mean_next = matvec(gain_now, mean_next) + offsets[step]
        cov_steps[step] = cov_next
        mean_steps[step] = mean_next
    return jnp.stack(mean_steps), jnp.stack(cov_steps)


def per_device(
    dynamics,
    dynamics_mask,
    obs_op,
    obs_mask,
    process_noise,
    initial_expectation,
    filter_gains,
    observations,
    smooth_gains,
    filt_cov,
):
    width = dynamics.shape[0]
    obs_width = obs_op.shape[0]
    row_count = filter_gains.shape[1]
    row_start = lax.axis_index("blk") * row_count
    trans_map = dynamics * expand_mask(dynamics_mask, width, width)
    obs_map = obs_op * expand_mask(obs_mask, obs_width, width)
    obs_dyn = matmul(obs_map, trans_map)
    own_rows = lax.dynamic_slice_in_dim(trans_map, row_start, row_count, 0)
    map_rows = own_rows[None] - matmul(filter_gains, obs_dyn)
    shift_rows = jnp.einsum("tro,to->tr", filter_gains, observations, precision=highest)
    def steps_whole(rows):
        return lax.all_to_all(rows, "blk", 0, 1, tiled=True)

    def rows_of_steps(whole):
        return lax.all_to_all(whole, "blk", 1, 0, tiled=True)

    means_out, cov_out = window_work(
        trans_map,
        process_noise,
        initial_expectation,
        steps_whole(map_rows),
        steps_whole(shift_rows),
        steps_whole(smooth_gains),
        steps_whole(filt_cov),
        lax.axis_index(CHUNKS),
        lax.axis_size(CHUNKS),
    )
    return (rows_of_steps(means_out), rows_of_steps(cov_out))


def solution(mesh):
    return jax.shard_map(
        per_device,
        mesh=mesh,
        in_specs=(
            P(),
            P(),
            P(),
            P(),
            P(),
            P(),
            P("tm", "blk", None),
            P("tm", None),
            P("tm", "blk", None),
            P("tm", "blk", None),
        ),
        out_specs=(P("tm", "blk"), P("tm", "blk", None)),
        check_vma=False,
    )
```

```python
import jax
import jax.numpy as jnp
from jax import lax
from jax.sharding import PartitionSpec as P

highest = lax.Precision.HIGHEST
CHUNKS = ("tm", "blk")


def from_behind(block, axis, distance):
    devices = range(lax.axis_size(axis))
    route = [(i - distance, i) for i in devices if i - distance in devices]
    return lax.ppermute(block, axis, route)


def expand_mask(mask, row_total, col_total):
    row_block = row_total // mask.shape[0]
    col_block = col_total // mask.shape[1]
    return jnp.repeat(jnp.repeat(mask.astype(jnp.float32), row_block, axis=0), col_block, axis=1)


def matmul(left, right):
    return jnp.matmul(left, right, precision=highest)


def matvec(left, right):
    return jnp.einsum("...ij,...j->...i", left, right, precision=highest)


def transpose(mats):
    return jnp.swapaxes(mats, -1, -2)


def filter_tree(maps, shifts):
    while maps.shape[0] > 1:
        early_map, late_map = maps[0::2], maps[1::2]
        shifts = matvec(late_map, shifts[0::2]) + shifts[1::2]
        maps = matmul(late_map, early_map)
    return maps[0], shifts[0]


def smooth_tree(gains, resids):
    levels = []
    while gains.shape[0] > 1:
        outer, inner = gains[0::2], gains[1::2]
        levels.append(outer)
        resids = matmul(matmul(outer, resids[1::2]), transpose(outer)) + resids[0::2]
        gains = matmul(outer, inner)
    return gains[0], resids[0], levels


def offset_tree(levels, offsets):
    for outer in levels:
        offsets = matvec(outer, offsets[1::2]) + offsets[0::2]
    return offsets[0]


def filter_scan(window_map, window_shift, initial_expectation, tm_index, tm_count):
    width = window_map.shape[0]
    first_window = tm_index == 0
    shift = jnp.where(first_window, matvec(window_map, initial_expectation) + window_shift, window_shift)
    cmap = jnp.where(first_window, jnp.float32(0.0), window_map)
    distance = 1
    while distance < tm_count:
        has_left = tm_index >= distance
        if 2 * distance >= tm_count:
            shift_left = from_behind(shift, CHUNKS, distance)
            shift = jnp.where(has_left, matvec(cmap, shift_left) + shift, shift)
        else:
            arrived = from_behind(jnp.concatenate([cmap, shift[None]], axis=0), CHUNKS, distance)
            map_left, shift_left = arrived[:width], arrived[width]
            shift = jnp.where(has_left, matvec(cmap, shift_left) + shift, shift)
            cmap = jnp.where(has_left, matmul(cmap, map_left), cmap)
        distance *= 2
    mean_in = from_behind(shift, CHUNKS, 1)
    return jnp.where(first_window, initial_expectation, mean_in)


def cov_scan(window_gain, window_resid, tm_index, tm_count):
    gain, resid = window_gain, window_resid
    round_gains = []
    distance = 1
    while 2 * distance < tm_count:
        has_right = tm_index + distance < tm_count
        round_gains.append(gain)
        resid_right = from_behind(resid, CHUNKS, -distance)
        gain_right = from_behind(gain, CHUNKS, -distance)
        new_resid = matmul(matmul(gain, resid_right), gain.T) + resid
        resid = jnp.where(has_right, new_resid, resid)
        gain = jnp.where(has_right, matmul(gain, gain_right), gain)
        distance *= 2
    round_gains.append(gain)
    gain_next = from_behind(gain, CHUNKS, -1)
    resid_next = from_behind(resid, CHUNKS, -1)
    resid_far = from_behind(resid, CHUNKS, -(distance + 1))
    has_far = tm_index + distance + 1 < tm_count
    cov_after = jnp.where(
        has_far, matmul(matmul(gain_next, resid_far), gain_next.T) + resid_next, resid_next
    )
    return jnp.where(tm_index == tm_count - 1, jnp.float32(0.0), cov_after), round_gains


def offset_scan(window_offset, round_gains, tm_index, tm_count):
    offset = window_offset
    distance = 1
    for gain in round_gains:
        has_right = tm_index + distance < tm_count
        offset_right = from_behind(offset, CHUNKS, -distance)
        offset = jnp.where(has_right, matvec(gain, offset_right) + offset, offset)
        distance *= 2
    mean_after = from_behind(offset, CHUNKS, -1)
    return jnp.where(tm_index == tm_count - 1, jnp.float32(0.0), mean_after)


def window_work(
    trans_map,
    process_noise,
    initial_expectation,
    transition_operators,
    step_shifts,
    gain_full,
    cov_full,
    tm_index,
    tm_count,
):
    step_count = transition_operators.shape[0]
    final_step = jnp.logical_and(tm_index == tm_count - 1, jnp.arange(step_count) == step_count - 1)
    gain_full = jnp.where(final_step[:, None, None], jnp.float32(0.0), gain_full)

    predicted = matmul(matmul(trans_map, cov_full), trans_map.T) + jnp.diag(process_noise)
    gain_trans = jnp.swapaxes(gain_full, 1, 2)
    residual_cov = cov_full - matmul(matmul(gain_full, predicted), gain_trans)
    window_gain, window_resid, gain_levels = smooth_tree(gain_full, residual_cov)
    cov_after, round_gains = cov_scan(window_gain, window_resid, tm_index, tm_count)

    window_map, window_shift = filter_tree(transition_operators, step_shifts)
    mean_in = filter_scan(window_map, window_shift, initial_expectation, tm_index, tm_count)

    filt_steps = []
    current = mean_in
    for step in range(step_count):
        current = matvec(transition_operators[step], current) + step_shifts[step]
        filt_steps.append(current)
    filt_means = jnp.stack(filt_steps)
    moved_means = jnp.einsum("ij,tj->ti", trans_map, filt_means, precision=highest)
    offsets = filt_means - jnp.einsum("tij,tj->ti", gain_full, moved_means, precision=highest)
    mean_after = offset_scan(offset_tree(gain_levels, offsets), round_gains, tm_index, tm_count)

    cov_steps = [None] * step_count
    mean_steps = [None] * step_count
    cov_next, mean_next = cov_after, mean_after
    for step in reversed(range(step_count)):
        gain_now = gain_full[step]
        cov_next = matmul(matmul(gain_now, cov_next), gain_now.T) + residual_cov[step]
        mean_next = matvec(gain_now, mean_next) + offsets[step]
        cov_steps[step] = cov_next
        mean_steps[step] = mean_next
    return jnp.stack(mean_steps), jnp.stack(cov_steps)


def per_device(
    dynamics,
    dynamics_mask,
    obs_op,
    obs_mask,
    process_noise,
    initial_expectation,
    filter_gains,
    observations,
    smooth_gains,
    filt_cov,
):
    width = dynamics.shape[0]
    obs_width = obs_op.shape[0]
    row_count = filter_gains.shape[1]
    row_start = lax.axis_index("blk") * row_count
    trans_map = dynamics * expand_mask(dynamics_mask, width, width)
    obs_map = obs_op * expand_mask(obs_mask, obs_width, width)
    obs_dyn = matmul(obs_map, trans_map)
    own_rows = lax.dynamic_slice_in_dim(trans_map, row_start, row_count, 0)
    map_rows = own_rows[None] - matmul(filter_gains, obs_dyn)
    shift_rows = jnp.einsum("tro,to->tr", filter_gains, observations, precision=highest)
    def steps_whole(rows):
        return lax.all_to_all(rows, "blk", 0, 1, tiled=True)

    def rows_of_steps(whole):
        return lax.all_to_all(whole, "blk", 1, 0, tiled=True)

    means_out, cov_out = window_work(
        trans_map,
        process_noise,
        initial_expectation,
        steps_whole(map_rows),
        steps_whole(shift_rows),
        steps_whole(smooth_gains),
        steps_whole(filt_cov),
        lax.axis_index(CHUNKS),
        lax.axis_size(CHUNKS),
    )
    return (rows_of_steps(means_out), rows_of_steps(cov_out))


def solution(mesh):
    return jax.shard_map(
        per_device,
        mesh=mesh,
        in_specs=(
            P(),
            P(),
            P(),
            P(),
            P(),
            P(),
            P("tm", "blk", None),
            P("tm", None),
            P("tm", "blk", None),
            P("tm", "blk", None),
        ),
        out_specs=(P("tm", "blk"), P("tm", "blk", None)),
        check_vma=False,
    )
```

```python
import jax
import jax.numpy as jnp
from jax import lax
from jax.sharding import PartitionSpec as P

highest = lax.Precision.HIGHEST
CHUNKS = ("tm", "blk")


def from_behind(block, axis, distance):
    devices = range(lax.axis_size(axis))
    route = [(i - distance, i) for i in devices if i - distance in devices]
    return lax.ppermute(block, axis, route)


def expand_mask(mask, row_total, col_total):
    row_block = row_total // mask.shape[0]
    col_block = col_total // mask.shape[1]
    return jnp.repeat(jnp.repeat(mask.astype(jnp.float32), row_block, axis=0), col_block, axis=1)


def matmul(left, right):
    return jnp.matmul(left, right, precision=highest)


def matvec(left, right):
    return jnp.einsum("...ij,...j->...i", left, right, precision=highest)


def transpose(mats):
    return jnp.swapaxes(mats, -1, -2)


def filter_tree(maps, shifts):
    while maps.shape[0] > 1:
        early_map, late_map = maps[0::2], maps[1::2]
        shifts = matvec(late_map, shifts[0::2]) + shifts[1::2]
        maps = matmul(late_map, early_map)
    return maps[0], shifts[0]


def smooth_tree(gains, resids):
    levels = []
    while gains.shape[0] > 1:
        outer, inner = gains[0::2], gains[1::2]
        levels.append(outer)
        resids = matmul(matmul(outer, resids[1::2]), transpose(outer)) + resids[0::2]
        gains = matmul(outer, inner)
    return gains[0], resids[0], levels


def offset_tree(levels, offsets):
    for outer in levels:
        offsets = matvec(outer, offsets[1::2]) + offsets[0::2]
    return offsets[0]


def filter_scan(window_map, window_shift, initial_expectation, tm_index, tm_count):
    width = window_map.shape[0]
    first_window = tm_index == 0
    shift = jnp.where(first_window, matvec(window_map, initial_expectation) + window_shift, window_shift)
    cmap = jnp.where(first_window, jnp.float32(0.0), window_map)
    distance = 1
    while distance < tm_count:
        has_left = tm_index >= distance
        if 2 * distance >= tm_count:
            shift_left = from_behind(shift, CHUNKS, distance)
            shift = jnp.where(has_left, matvec(cmap, shift_left) + shift, shift)
        else:
            arrived = from_behind(jnp.concatenate([cmap, shift[None]], axis=0), CHUNKS, distance)
            map_left, shift_left = arrived[:width], arrived[width]
            shift = jnp.where(has_left, matvec(cmap, shift_left) + shift, shift)
            cmap = jnp.where(has_left, matmul(cmap, map_left), cmap)
        distance *= 2
    mean_in = from_behind(shift, CHUNKS, 1)
    return jnp.where(first_window, initial_expectation, mean_in)


def cov_scan(window_gain, window_resid, tm_index, tm_count):
    gain, resid = window_gain, window_resid
    round_gains = []
    distance = 1
    while 2 * distance < tm_count:
        has_right = tm_index + distance < tm_count
        round_gains.append(gain)
        resid_right = from_behind(resid, CHUNKS, -distance)
        gain_right = from_behind(gain, CHUNKS, -distance)
        new_resid = matmul(matmul(gain, resid_right), gain.T) + resid
        resid = jnp.where(has_right, new_resid, resid)
        gain = jnp.where(has_right, matmul(gain, gain_right), gain)
        distance *= 2
    round_gains.append(gain)
    gain_next = from_behind(gain, CHUNKS, -1)
    resid_next = from_behind(resid, CHUNKS, -1)
    resid_far = from_behind(resid, CHUNKS, -(distance + 1))
    has_far = tm_index + distance + 1 < tm_count
    cov_after = jnp.where(
        has_far, matmul(matmul(gain_next, resid_far), gain_next.T) + resid_next, resid_next
    )
    return jnp.where(tm_index == tm_count - 1, jnp.float32(0.0), cov_after), round_gains, gain_next


def offset_scan(window_offset, round_gains, gain_next, tm_index, tm_count):
    offset = window_offset
    distance = 1
    for gain in round_gains[:-1]:
        has_right = tm_index + distance < tm_count
        offset_right = from_behind(offset, CHUNKS, -distance)
        offset = jnp.where(has_right, matvec(gain, offset_right) + offset, offset)
        distance *= 2
    offset_next = from_behind(offset, CHUNKS, -1)
    offset_far = from_behind(offset, CHUNKS, -(distance + 1))
    has_far = tm_index + distance + 1 < tm_count
    mean_after = jnp.where(has_far, matvec(gain_next, offset_far) + offset_next, offset_next)
    return jnp.where(tm_index == tm_count - 1, jnp.float32(0.0), mean_after)


def window_work(
    trans_map,
    process_noise,
    initial_expectation,
    transition_operators,
    step_shifts,
    gain_full,
    cov_full,
    tm_index,
    tm_count,
):
    step_count = transition_operators.shape[0]
    final_step = jnp.logical_and(tm_index == tm_count - 1, jnp.arange(step_count) == step_count - 1)
    gain_full = jnp.where(final_step[:, None, None], jnp.float32(0.0), gain_full)

    predicted = matmul(matmul(trans_map, cov_full), trans_map.T) + jnp.diag(process_noise)
    gain_trans = jnp.swapaxes(gain_full, 1, 2)
    residual_cov = cov_full - matmul(matmul(gain_full, predicted), gain_trans)
    window_gain, window_resid, gain_levels = smooth_tree(gain_full, residual_cov)
    cov_after, round_gains, gain_next = cov_scan(window_gain, window_resid, tm_index, tm_count)

    window_map, window_shift = filter_tree(transition_operators, step_shifts)
    mean_in = filter_scan(window_map, window_shift, initial_expectation, tm_index, tm_count)

    filt_steps = []
    current = mean_in
    for step in range(step_count):
        current = matvec(transition_operators[step], current) + step_shifts[step]
        filt_steps.append(current)
    filt_means = jnp.stack(filt_steps)
    moved_means = jnp.einsum("ij,tj->ti", trans_map, filt_means, precision=highest)
    offsets = filt_means - jnp.einsum("tij,tj->ti", gain_full, moved_means, precision=highest)
    mean_after = offset_scan(
        offset_tree(gain_levels, offsets), round_gains, gain_next, tm_index, tm_count
    )

    cov_steps = [None] * step_count
    mean_steps = [None] * step_count
    cov_next, mean_next = cov_after, mean_after
    for step in reversed(range(step_count)):
        gain_now = gain_full[step]
        cov_next = matmul(matmul(gain_now, cov_next), gain_now.T) + residual_cov[step]
        mean_next = matvec(gain_now, mean_next) + offsets[step]
        cov_steps[step] = cov_next
        mean_steps[step] = mean_next
    return jnp.stack(mean_steps), jnp.stack(cov_steps)


def per_device(
    dynamics,
    dynamics_mask,
    obs_op,
    obs_mask,
    process_noise,
    initial_expectation,
    filter_gains,
    observations,
    smooth_gains,
    filt_cov,
):
    width = dynamics.shape[0]
    obs_width = obs_op.shape[0]
    row_count = filter_gains.shape[1]
    row_start = lax.axis_index("blk") * row_count
    trans_map = dynamics * expand_mask(dynamics_mask, width, width)
    obs_map = obs_op * expand_mask(obs_mask, obs_width, width)
    obs_dyn = matmul(obs_map, trans_map)
    own_rows = lax.dynamic_slice_in_dim(trans_map, row_start, row_count, 0)
    map_rows = own_rows[None] - matmul(filter_gains, obs_dyn)
    shift_rows = jnp.einsum("tro,to->tr", filter_gains, observations, precision=highest)
    def steps_whole(rows):
        return lax.all_to_all(rows, "blk", 0, 1, tiled=True)

    def rows_of_steps(whole):
        return lax.all_to_all(whole, "blk", 1, 0, tiled=True)

    means_out, cov_out = window_work(
        trans_map,
        process_noise,
        initial_expectation,
        steps_whole(map_rows),
        steps_whole(shift_rows),
        steps_whole(smooth_gains),
        steps_whole(filt_cov),
        lax.axis_index(CHUNKS),
        lax.axis_size(CHUNKS),
    )
    return (rows_of_steps(means_out), rows_of_steps(cov_out))


def solution(mesh):
    return jax.shard_map(
        per_device,
        mesh=mesh,
        in_specs=(
            P(),
            P(),
            P(),
            P(),
            P(),
            P(),
            P("tm", "blk", None),
            P("tm", None),
            P("tm", "blk", None),
            P("tm", "blk", None),
        ),
        out_specs=(P("tm", "blk"), P("tm", "blk", None)),
        check_vma=False,
    )
```

```python
import jax
import jax.numpy as jnp
from jax import lax
from jax.sharding import PartitionSpec as P

highest = lax.Precision.HIGHEST
CHUNKS = ("tm", "blk")


def from_behind(block, axis, distance):
    devices = range(lax.axis_size(axis))
    route = [(i - distance, i) for i in devices if i - distance in devices]
    return lax.ppermute(block, axis, route)


def expand_mask(mask, row_total, col_total):
    row_block = row_total // mask.shape[0]
    col_block = col_total // mask.shape[1]
    return jnp.repeat(jnp.repeat(mask.astype(jnp.float32), row_block, axis=0), col_block, axis=1)


def matmul(left, right):
    return jnp.matmul(left, right, precision=highest)


def matvec(left, right):
    return jnp.einsum("...ij,...j->...i", left, right, precision=highest)


def transpose(mats):
    return jnp.swapaxes(mats, -1, -2)


def filter_tree(maps, shifts):
    while maps.shape[0] > 1:
        early_map, late_map = maps[0::2], maps[1::2]
        shifts = matvec(late_map, shifts[0::2]) + shifts[1::2]
        maps = matmul(late_map, early_map)
    return maps[0], shifts[0]


def smooth_tree(gains, resids):
    levels = []
    while gains.shape[0] > 1:
        outer, inner = gains[0::2], gains[1::2]
        levels.append(outer)
        resids = matmul(matmul(outer, resids[1::2]), transpose(outer)) + resids[0::2]
        gains = matmul(outer, inner)
    return gains[0], resids[0], levels


def offset_tree(levels, offsets):
    for outer in levels:
        offsets = matvec(outer, offsets[1::2]) + offsets[0::2]
    return offsets[0]


def filter_scan(window_map, window_shift, initial_expectation, tm_index, tm_count):
    width = window_map.shape[0]
    first_window = tm_index == 0
    shift = jnp.where(first_window, matvec(window_map, initial_expectation) + window_shift, window_shift)
    cmap = jnp.where(first_window, jnp.float32(0.0), window_map)
    distance = 1
    while distance < tm_count:
        has_left = tm_index >= distance
        if 2 * distance >= tm_count:
            shift_left = from_behind(shift, CHUNKS, distance)
            shift = jnp.where(has_left, matvec(cmap, shift_left) + shift, shift)
        else:
            arrived = from_behind(jnp.concatenate([cmap, shift[None]], axis=0), CHUNKS, distance)
            map_left, shift_left = arrived[:width], arrived[width]
            shift = jnp.where(has_left, matvec(cmap, shift_left) + shift, shift)
            cmap = jnp.where(has_left, matmul(cmap, map_left), cmap)
        distance *= 2
    mean_in = from_behind(shift, CHUNKS, 1)
    return jnp.where(first_window, initial_expectation, mean_in)


def cov_scan(window_gain, window_resid, tm_index, tm_count):
    gain, resid = window_gain, window_resid
    round_gains = []
    distance = 1
    while 2 * distance < tm_count:
        has_right = tm_index + distance < tm_count
        round_gains.append(gain)
        resid_right = from_behind(resid, CHUNKS, -distance)
        gain_right = from_behind(gain, CHUNKS, -distance)
        new_resid = matmul(matmul(gain, resid_right), gain.T) + resid
        resid = jnp.where(has_right, new_resid, resid)
        gain = jnp.where(has_right, matmul(gain, gain_right), gain)
        distance *= 2
    round_gains.append(gain)
    gain_next = from_behind(gain, CHUNKS, -1)
    resid_next = from_behind(resid, CHUNKS, -1)
    resid_far = from_behind(resid, CHUNKS, -(distance + 1))
    has_far = tm_index + distance + 1 < tm_count
    cov_after = jnp.where(
        has_far, matmul(matmul(gain_next, resid_far), gain_next.T) + resid_next, resid_next
    )
    return jnp.where(tm_index == tm_count - 1, jnp.float32(0.0), cov_after), round_gains


def offset_scan(window_offset, round_gains, tm_index, tm_count):
    offset = window_offset
    distance = 1
    for gain in round_gains:
        has_right = tm_index + distance < tm_count
        offset_right = from_behind(offset, CHUNKS, -distance)
        offset = jnp.where(has_right, matvec(gain, offset_right) + offset, offset)
        distance *= 2
    mean_after = from_behind(offset, CHUNKS, -1)
    return jnp.where(tm_index == tm_count - 1, jnp.float32(0.0), mean_after)


def window_work(
    trans_map,
    process_noise,
    initial_expectation,
    transition_operators,
    step_shifts,
    gain_full,
    cov_full,
    tm_index,
    tm_count,
):
    step_count = transition_operators.shape[0]
    final_step = jnp.logical_and(tm_index == tm_count - 1, jnp.arange(step_count) == step_count - 1)
    gain_full = jnp.where(final_step[:, None, None], jnp.float32(0.0), gain_full)

    predicted = matmul(matmul(trans_map, cov_full), trans_map.T) + jnp.diag(process_noise)
    gain_trans = jnp.swapaxes(gain_full, 1, 2)
    residual_cov = cov_full - matmul(matmul(gain_full, predicted), gain_trans)
    window_gain, window_resid, gain_levels = smooth_tree(gain_full, residual_cov)
    cov_after, round_gains = cov_scan(window_gain, window_resid, tm_index, tm_count)

    window_map, window_shift = filter_tree(transition_operators, step_shifts)
    mean_in = filter_scan(window_map, window_shift, initial_expectation, tm_index, tm_count)

    filt_steps = []
    current = mean_in
    for step in range(step_count):
        current = matvec(transition_operators[step], current) + step_shifts[step]
        filt_steps.append(current)
    filt_means = jnp.stack(filt_steps)
    moved_means = jnp.einsum("ij,tj->ti", trans_map, filt_means, precision=highest)
    offsets = filt_means - jnp.einsum("tij,tj->ti", gain_full, moved_means, precision=highest)
    mean_after = offset_scan(offset_tree(gain_levels, offsets), round_gains, tm_index, tm_count)

    cov_steps = [None] * step_count
    mean_steps = [None] * step_count
    cov_next, mean_next = cov_after, mean_after
    for step in reversed(range(step_count)):
        gain_now = gain_full[step]
        cov_next = matmul(matmul(gain_now, cov_next), gain_now.T) + residual_cov[step]
        mean_next = matvec(gain_now, mean_next) + offsets[step]
        cov_steps[step] = cov_next
        mean_steps[step] = mean_next
    return jnp.stack(mean_steps), jnp.stack(cov_steps)


def per_device(
    dynamics,
    dynamics_mask,
    obs_op,
    obs_mask,
    process_noise,
    initial_expectation,
    filter_gains,
    observations,
    smooth_gains,
    filt_cov,
):
    width = dynamics.shape[0]
    obs_width = obs_op.shape[0]
    row_count = filter_gains.shape[1]
    row_start = lax.axis_index("blk") * row_count
    trans_map = dynamics * expand_mask(dynamics_mask, width, width)
    obs_map = obs_op * expand_mask(obs_mask, obs_width, width)
    obs_dyn = matmul(obs_map, trans_map)
    own_rows = lax.dynamic_slice_in_dim(trans_map, row_start, row_count, 0)
    map_rows = own_rows[None] - matmul(filter_gains, obs_dyn)
    shift_rows = jnp.einsum("tro,to->tr", filter_gains, observations, precision=highest)
    def steps_whole(rows):
        return lax.all_to_all(rows, "blk", 0, 1, tiled=True)

    def rows_of_steps(whole):
        return lax.all_to_all(whole, "blk", 1, 0, tiled=True)

    map_whole = steps_whole(map_rows)
    shift_whole = steps_whole(shift_rows)
    map_whole, shift_whole, smooth_gains, filt_cov = lax.optimization_barrier(
        (map_whole, shift_whole, smooth_gains, filt_cov)
    )
    means_out, cov_out = window_work(
        trans_map,
        process_noise,
        initial_expectation,
        map_whole,
        shift_whole,
        steps_whole(smooth_gains),
        steps_whole(filt_cov),
        lax.axis_index(CHUNKS),
        lax.axis_size(CHUNKS),
    )
    return (rows_of_steps(means_out), rows_of_steps(cov_out))


def solution(mesh):
    return jax.shard_map(
        per_device,
        mesh=mesh,
        in_specs=(
            P(),
            P(),
            P(),
            P(),
            P(),
            P(),
            P("tm", "blk", None),
            P("tm", None),
            P("tm", "blk", None),
            P("tm", "blk", None),
        ),
        out_specs=(P("tm", "blk"), P("tm", "blk", None)),
        check_vma=False,
    )
```

```python
import jax
import jax.numpy as jnp
from jax import lax
from jax.sharding import PartitionSpec as P

highest = lax.Precision.HIGHEST
CHUNKS = ("tm", "blk")


def from_behind(block, axis, distance):
    devices = range(lax.axis_size(axis))
    route = [(i - distance, i) for i in devices if i - distance in devices]
    return lax.ppermute(block, axis, route)


def expand_mask(mask, row_total, col_total):
    row_block = row_total // mask.shape[0]
    col_block = col_total // mask.shape[1]
    return jnp.repeat(jnp.repeat(mask.astype(jnp.float32), row_block, axis=0), col_block, axis=1)


def matmul(left, right):
    return jnp.matmul(left, right, precision=highest)


def matvec(left, right):
    return jnp.einsum("...ij,...j->...i", left, right, precision=highest)


def transpose(mats):
    return jnp.swapaxes(mats, -1, -2)


def filter_tree(maps, shifts):
    while maps.shape[0] > 1:
        early_map, late_map = maps[0::2], maps[1::2]
        shifts = matvec(late_map, shifts[0::2]) + shifts[1::2]
        maps = matmul(late_map, early_map)
    return maps[0], shifts[0]


def smooth_tree(gains, resids):
    levels = []
    while gains.shape[0] > 1:
        outer, inner = gains[0::2], gains[1::2]
        levels.append(outer)
        resids = matmul(matmul(outer, resids[1::2]), transpose(outer)) + resids[0::2]
        gains = matmul(outer, inner)
    return gains[0], resids[0], levels


def offset_tree(levels, offsets):
    for outer in levels:
        offsets = matvec(outer, offsets[1::2]) + offsets[0::2]
    return offsets[0]


def filter_scan(window_map, window_shift, initial_expectation, tm_index, tm_count):
    width = window_map.shape[0]
    first_window = tm_index == 0
    shift = jnp.where(first_window, matvec(window_map, initial_expectation) + window_shift, window_shift)
    cmap = jnp.where(first_window, jnp.float32(0.0), window_map)
    distance = 1
    while distance < tm_count:
        has_left = tm_index >= distance
        if 2 * distance >= tm_count:
            shift_left = from_behind(shift, CHUNKS, distance)
            shift = jnp.where(has_left, matvec(cmap, shift_left) + shift, shift)
        else:
            arrived = from_behind(jnp.concatenate([cmap, shift[None]], axis=0), CHUNKS, distance)
            map_left, shift_left = arrived[:width], arrived[width]
            shift = jnp.where(has_left, matvec(cmap, shift_left) + shift, shift)
            cmap = jnp.where(has_left, matmul(cmap, map_left), cmap)
        distance *= 2
    mean_in = from_behind(shift, CHUNKS, 1)
    return jnp.where(first_window, initial_expectation, mean_in)


def cov_scan(window_gain, window_resid, tm_index, tm_count):
    gain, resid = window_gain, window_resid
    round_gains = []
    distance = 1
    while 2 * distance < tm_count:
        has_right = tm_index + distance < tm_count
        round_gains.append(gain)
        resid_right = from_behind(resid, CHUNKS, -distance)
        gain_right = from_behind(gain, CHUNKS, -distance)
        new_resid = matmul(matmul(gain, resid_right), gain.T) + resid
        resid = jnp.where(has_right, new_resid, resid)
        gain = jnp.where(has_right, matmul(gain, gain_right), gain)
        distance *= 2
    round_gains.append(gain)
    return gain, resid, distance, round_gains


def cov_finish(gain, resid, distance, tm_index, tm_count):
    gain_next = from_behind(gain, CHUNKS, -1)
    resid_next = from_behind(resid, CHUNKS, -1)
    resid_far = from_behind(resid, CHUNKS, -(distance + 1))
    has_far = tm_index + distance + 1 < tm_count
    cov_after = jnp.where(
        has_far, matmul(matmul(gain_next, resid_far), gain_next.T) + resid_next, resid_next
    )
    return jnp.where(tm_index == tm_count - 1, jnp.float32(0.0), cov_after)


def offset_scan(window_offset, round_gains, tm_index, tm_count):
    offset = window_offset
    distance = 1
    for gain in round_gains:
        has_right = tm_index + distance < tm_count
        offset_right = from_behind(offset, CHUNKS, -distance)
        offset = jnp.where(has_right, matvec(gain, offset_right) + offset, offset)
        distance *= 2
    mean_after = from_behind(offset, CHUNKS, -1)
    return jnp.where(tm_index == tm_count - 1, jnp.float32(0.0), mean_after)


def window_work(
    trans_map,
    process_noise,
    initial_expectation,
    transition_operators,
    step_shifts,
    gain_full,
    cov_full,
    tm_index,
    tm_count,
):
    step_count = transition_operators.shape[0]
    final_step = jnp.logical_and(tm_index == tm_count - 1, jnp.arange(step_count) == step_count - 1)
    gain_full = jnp.where(final_step[:, None, None], jnp.float32(0.0), gain_full)

    predicted = matmul(matmul(trans_map, cov_full), trans_map.T) + jnp.diag(process_noise)
    gain_trans = jnp.swapaxes(gain_full, 1, 2)
    residual_cov = cov_full - matmul(matmul(gain_full, predicted), gain_trans)
    window_gain, window_resid, gain_levels = smooth_tree(gain_full, residual_cov)
    scan_gain, scan_resid, distance, round_gains = cov_scan(window_gain, window_resid, tm_index, tm_count)

    window_map, window_shift = filter_tree(transition_operators, step_shifts)
    mean_in = filter_scan(window_map, window_shift, initial_expectation, tm_index, tm_count)

    filt_steps = []
    current = mean_in
    for step in range(step_count):
        current = matvec(transition_operators[step], current) + step_shifts[step]
        filt_steps.append(current)
    filt_means = jnp.stack(filt_steps)
    moved_means = jnp.einsum("ij,tj->ti", trans_map, filt_means, precision=highest)
    offsets = filt_means - jnp.einsum("tij,tj->ti", gain_full, moved_means, precision=highest)
    mean_after = offset_scan(offset_tree(gain_levels, offsets), round_gains, tm_index, tm_count)
    scan_gain, scan_resid, mean_after = lax.optimization_barrier((scan_gain, scan_resid, mean_after))
    cov_after = cov_finish(scan_gain, scan_resid, distance, tm_index, tm_count)

    cov_steps = [None] * step_count
    mean_steps = [None] * step_count
    cov_next, mean_next = cov_after, mean_after
    for step in reversed(range(step_count)):
        gain_now = gain_full[step]
        cov_next = matmul(matmul(gain_now, cov_next), gain_now.T) + residual_cov[step]
        mean_next = matvec(gain_now, mean_next) + offsets[step]
        cov_steps[step] = cov_next
        mean_steps[step] = mean_next
    return jnp.stack(mean_steps), jnp.stack(cov_steps)


def per_device(
    dynamics,
    dynamics_mask,
    obs_op,
    obs_mask,
    process_noise,
    initial_expectation,
    filter_gains,
    observations,
    smooth_gains,
    filt_cov,
):
    width = dynamics.shape[0]
    obs_width = obs_op.shape[0]
    row_count = filter_gains.shape[1]
    row_start = lax.axis_index("blk") * row_count
    trans_map = dynamics * expand_mask(dynamics_mask, width, width)
    obs_map = obs_op * expand_mask(obs_mask, obs_width, width)
    obs_dyn = matmul(obs_map, trans_map)
    own_rows = lax.dynamic_slice_in_dim(trans_map, row_start, row_count, 0)
    map_rows = own_rows[None] - matmul(filter_gains, obs_dyn)
    shift_rows = jnp.einsum("tro,to->tr", filter_gains, observations, precision=highest)
    def steps_whole(rows):
        return lax.all_to_all(rows, "blk", 0, 1, tiled=True)

    def rows_of_steps(whole):
        return lax.all_to_all(whole, "blk", 1, 0, tiled=True)

    means_out, cov_out = window_work(
        trans_map,
        process_noise,
        initial_expectation,
        steps_whole(map_rows),
        steps_whole(shift_rows),
        steps_whole(smooth_gains),
        steps_whole(filt_cov),
        lax.axis_index(CHUNKS),
        lax.axis_size(CHUNKS),
    )
    return (rows_of_steps(means_out), rows_of_steps(cov_out))


def solution(mesh):
    return jax.shard_map(
        per_device,
        mesh=mesh,
        in_specs=(
            P(),
            P(),
            P(),
            P(),
            P(),
            P(),
            P("tm", "blk", None),
            P("tm", None),
            P("tm", "blk", None),
            P("tm", "blk", None),
        ),
        out_specs=(P("tm", "blk"), P("tm", "blk", None)),
        check_vma=False,
    )
```

```python
import jax
import jax.numpy as jnp
from jax import lax
from jax.sharding import PartitionSpec as P

highest = lax.Precision.HIGHEST
CHUNKS = ("tm", "blk")


def from_behind(block, axis, distance):
    devices = range(lax.axis_size(axis))
    route = [(i - distance, i) for i in devices if i - distance in devices]
    return lax.ppermute(block, axis, route)


def expand_mask(mask, row_total, col_total):
    row_block = row_total // mask.shape[0]
    col_block = col_total // mask.shape[1]
    return jnp.repeat(jnp.repeat(mask.astype(jnp.float32), row_block, axis=0), col_block, axis=1)


def matmul(left, right):
    return jnp.matmul(left, right, precision=highest)


def matvec(left, right):
    return jnp.einsum("...ij,...j->...i", left, right, precision=highest)


def transpose(mats):
    return jnp.swapaxes(mats, -1, -2)


def filter_tree(maps, shifts):
    while maps.shape[0] > 1:
        early_map, late_map = maps[0::2], maps[1::2]
        shifts = matvec(late_map, shifts[0::2]) + shifts[1::2]
        maps = matmul(late_map, early_map)
    return maps[0], shifts[0]


def smooth_tree(gains, resids):
    levels = []
    while gains.shape[0] > 1:
        outer, inner = gains[0::2], gains[1::2]
        levels.append(outer)
        resids = matmul(matmul(outer, resids[1::2]), transpose(outer)) + resids[0::2]
        gains = matmul(outer, inner)
    return gains[0], resids[0], levels


def offset_tree(levels, offsets):
    for outer in levels:
        offsets = matvec(outer, offsets[1::2]) + offsets[0::2]
    return offsets[0]


def filter_scan(window_map, window_shift, initial_expectation, tm_index, tm_count):
    width = window_map.shape[0]
    first_window = tm_index == 0
    shift = jnp.where(first_window, matvec(window_map, initial_expectation) + window_shift, window_shift)
    cmap = jnp.where(first_window, jnp.float32(0.0), window_map)
    distance = 1
    while distance < tm_count:
        has_left = tm_index >= distance
        if 2 * distance >= tm_count:
            shift_left = from_behind(shift, CHUNKS, distance)
            shift = jnp.where(has_left, matvec(cmap, shift_left) + shift, shift)
        else:
            tail = jnp.zeros((7, width), jnp.float32)
            arrived = from_behind(jnp.concatenate([cmap, shift[None], tail], axis=0), CHUNKS, distance)
            map_left, shift_left = arrived[:width], arrived[width]
            shift = jnp.where(has_left, matvec(cmap, shift_left) + shift, shift)
            cmap = jnp.where(has_left, matmul(cmap, map_left), cmap)
        distance *= 2
    mean_in = from_behind(shift, CHUNKS, 1)
    return jnp.where(first_window, initial_expectation, mean_in)


def cov_scan(window_gain, window_resid, tm_index, tm_count):
    gain, resid = window_gain, window_resid
    round_gains = []
    distance = 1
    while 2 * distance < tm_count:
        has_right = tm_index + distance < tm_count
        round_gains.append(gain)
        resid_right = from_behind(resid, CHUNKS, -distance)
        gain_right = from_behind(gain, CHUNKS, -distance)
        new_resid = matmul(matmul(gain, resid_right), gain.T) + resid
        resid = jnp.where(has_right, new_resid, resid)
        gain = jnp.where(has_right, matmul(gain, gain_right), gain)
        distance *= 2
    round_gains.append(gain)
    gain_next = from_behind(gain, CHUNKS, -1)
    resid_next = from_behind(resid, CHUNKS, -1)
    resid_far = from_behind(resid, CHUNKS, -(distance + 1))
    has_far = tm_index + distance + 1 < tm_count
    cov_after = jnp.where(
        has_far, matmul(matmul(gain_next, resid_far), gain_next.T) + resid_next, resid_next
    )
    return jnp.where(tm_index == tm_count - 1, jnp.float32(0.0), cov_after), round_gains


def offset_scan(window_offset, round_gains, tm_index, tm_count):
    offset = window_offset
    distance = 1
    for gain in round_gains:
        has_right = tm_index + distance < tm_count
        offset_right = from_behind(offset, CHUNKS, -distance)
        offset = jnp.where(has_right, matvec(gain, offset_right) + offset, offset)
        distance *= 2
    mean_after = from_behind(offset, CHUNKS, -1)
    return jnp.where(tm_index == tm_count - 1, jnp.float32(0.0), mean_after)


def window_work(
    trans_map,
    process_noise,
    initial_expectation,
    transition_operators,
    step_shifts,
    gain_full,
    cov_full,
    tm_index,
    tm_count,
):
    step_count = transition_operators.shape[0]
    final_step = jnp.logical_and(tm_index == tm_count - 1, jnp.arange(step_count) == step_count - 1)
    gain_full = jnp.where(final_step[:, None, None], jnp.float32(0.0), gain_full)

    predicted = matmul(matmul(trans_map, cov_full), trans_map.T) + jnp.diag(process_noise)
    gain_trans = jnp.swapaxes(gain_full, 1, 2)
    residual_cov = cov_full - matmul(matmul(gain_full, predicted), gain_trans)
    window_gain, window_resid, gain_levels = smooth_tree(gain_full, residual_cov)
    cov_after, round_gains = cov_scan(window_gain, window_resid, tm_index, tm_count)

    window_map, window_shift = filter_tree(transition_operators, step_shifts)
    mean_in = filter_scan(window_map, window_shift, initial_expectation, tm_index, tm_count)

    filt_steps = []
    current = mean_in
    for step in range(step_count):
        current = matvec(transition_operators[step], current) + step_shifts[step]
        filt_steps.append(current)
    filt_means = jnp.stack(filt_steps)
    moved_means = jnp.einsum("ij,tj->ti", trans_map, filt_means, precision=highest)
    offsets = filt_means - jnp.einsum("tij,tj->ti", gain_full, moved_means, precision=highest)
    mean_after = offset_scan(offset_tree(gain_levels, offsets), round_gains, tm_index, tm_count)

    cov_steps = [None] * step_count
    mean_steps = [None] * step_count
    cov_next, mean_next = cov_after, mean_after
    for step in reversed(range(step_count)):
        gain_now = gain_full[step]
        cov_next = matmul(matmul(gain_now, cov_next), gain_now.T) + residual_cov[step]
        mean_next = matvec(gain_now, mean_next) + offsets[step]
        cov_steps[step] = cov_next
        mean_steps[step] = mean_next
    return jnp.stack(mean_steps), jnp.stack(cov_steps)


def per_device(
    dynamics,
    dynamics_mask,
    obs_op,
    obs_mask,
    process_noise,
    initial_expectation,
    filter_gains,
    observations,
    smooth_gains,
    filt_cov,
):
    width = dynamics.shape[0]
    obs_width = obs_op.shape[0]
    row_count = filter_gains.shape[1]
    row_start = lax.axis_index("blk") * row_count
    trans_map = dynamics * expand_mask(dynamics_mask, width, width)
    obs_map = obs_op * expand_mask(obs_mask, obs_width, width)
    obs_dyn = matmul(obs_map, trans_map)
    own_rows = lax.dynamic_slice_in_dim(trans_map, row_start, row_count, 0)
    map_rows = own_rows[None] - matmul(filter_gains, obs_dyn)
    shift_rows = jnp.einsum("tro,to->tr", filter_gains, observations, precision=highest)
    def steps_whole(rows):
        return lax.all_to_all(rows, "blk", 0, 1, tiled=True)

    def rows_of_steps(whole):
        return lax.all_to_all(whole, "blk", 1, 0, tiled=True)

    means_out, cov_out = window_work(
        trans_map,
        process_noise,
        initial_expectation,
        steps_whole(map_rows),
        steps_whole(shift_rows),
        steps_whole(smooth_gains),
        steps_whole(filt_cov),
        lax.axis_index(CHUNKS),
        lax.axis_size(CHUNKS),
    )
    return (rows_of_steps(means_out), rows_of_steps(cov_out))


def solution(mesh):
    return jax.shard_map(
        per_device,
        mesh=mesh,
        in_specs=(
            P(),
            P(),
            P(),
            P(),
            P(),
            P(),
            P("tm", "blk", None),
            P("tm", None),
            P("tm", "blk", None),
            P("tm", "blk", None),
        ),
        out_specs=(P("tm", "blk"), P("tm", "blk", None)),
        check_vma=False,
    )
```
